128 devices in a mesh: line: 8 (over z, core), slab: 16 (over y, x).
Axes of the slice: x: 4, y: 4, z: 4, core: 2. Of those that a mesh axis runs over, the one named last changes fastest.
Arguments:
- mass_per_volume: float32 [4096, 2048], P('line', 'slab'), may hold values from 0.5 to 2
- fluid_speed_field: float32 [3, 4096, 2048], P(None, 'line', 'slab'), may hold values from -3 to 3
- fluid_thrust_field: float32 [4096, 2048], P('line', 'slab'), may hold values from 0.5 to 2
- shock_damping_field: float32 [4096, 2048], P('line', 'slab'), may hold values from 0.05 to 2
- grain_holding_processor: int32 [1048576, 1], P(('line', 'slab')), may hold values from 0 to 127; in each aligned block of 8192 rows (0 to 8191, 8192 to 16383, ...) at most 256 rows name the same one
- grain_mesh_slot: int32 [1048576], P(('line', 'slab')), may hold values from 0 to 65535
- grain_speed_vector: float32 [3, 1048576], P(None, ('line', 'slab')), may hold values from -3 to 3
- fluid_speed_at_grain: float32 [3, 1048576], P(None, ('line', 'slab')), may hold values from -3 to 3
- thermal_states: float32 [2, 1048576], P(None, ('line', 'slab')), may hold values from 0.5 to 2
- grain_mass_over_lag: float32 [1048576], P(('line', 'slab')), may hold values from 0.5 to 4
Outputs:
- gas_rate: float32 [5, 4096, 2048], P(None, 'line', 'slab')
The draws below stay inside these ranges and needn't reach their ends.
Inputs may be any that keep to these rules, and one draw needn't show every extreme that they name: `grain_holding_processor`: within the rows of one device, each destination device is named at most 256 times, and in some device's rows some destination is named exactly 256 times.
All inputs are finite; a program needn't handle non-finite values.
Results may differ from the reference program's by a relative error of at most 0.0003.
Values sent between devices are 32-bit elements; how exact they have to be, the bound alone decides.
No kernel may reach another device: no remote copies, remote signals or barrier semaphores. Data moves between devices by JAX's collectives and lax.ppermute only.
A program may use at most 64 MiB of HBM per device.

```python
import math
import jax
import jax.numpy as jnp
import numpy as np
from jax import lax

CX = 512
LINES_DEV = 128
PART_DEV = 8192
NX = 4096
NL = 2048
GRAIN_COUNT_ALL = 1048576
CAP = 256
N_SLAB = 16
DEVICES = 128


def touch_ends(entries, key, low, largest):
    longest = entries.shape.index(max(entries.shape))
    spots = []
    for shift in (0, 1):
        where = [jax.random.randint(jax.random.fold_in(key, axis), (), 0, length) for axis, length in enumerate(entries.shape)]
        where[longest] = (where[longest] + shift) % entries.shape[longest]
        spots.append(tuple(where))
    return entries.at[spots[0]].set(low).at[spots[1]].set(largest)


def steps_of(own_key, extent, shards, smallest, top_value):
    def one(position, blocks):
        steps = jax.random.uniform(jax.random.fold_in(jax.random.fold_in(own_key, 6), position), (blocks,), jnp.float32, smallest / len(shards), top_value / len(shards))
        return jnp.repeat(jnp.exp(steps), extent[position] // blocks).reshape((-1,) + (1,) * (len(extent) - position - 1))

    loudness = one(*shards[0])
    for cut in shards[1:]:
        loudness = loudness * one(*cut)
    return loudness


def assign_block(rng, own, number, rows, count, top, reach, lean):
    order = jax.random.permutation(rng, count)
    heavy_load, common = shares(count, rows * top, reach, lean, True), shares(count, rows * top, reach, lean, False)
    places = jnp.arange(count)

    def named(sizes, offset_by):
        used = int((sizes > 0).sum())
        fixed = max(1, used // 4)
        shifted = fixed + (places - fixed + offset_by * (used - fixed)) % max(1, count - fixed)
        return jnp.zeros((count,), jnp.int32).at[order[jnp.where(places < fixed, places, shifted)]].set(jnp.asarray(sizes, jnp.int32))

    sizes = jnp.where(number % 4 == 0, named(heavy_load, number // 4), named(common, number - number // 4 - 1))
    mixed = jax.random.permutation(jax.random.fold_in(own, 3), count)
    donor, receiver = mixed[0:count // 2 * 2:2], mixed[1:count // 2 * 2:2]
    margin = jnp.minimum(sizes[donor] - 1, reach - sizes[receiver]) // 2
    margin = jnp.where((donor == order[0]) | (receiver == order[0]) | (sizes[receiver] == 0), 0, jnp.maximum(margin, 0))
    shifted = jax.random.randint(jax.random.fold_in(own, 4), (count // 2,), 0, 1 << 20) % (margin + 1)
    sizes = sizes.at[donor].add(-shifted).at[receiver].add(shifted)
    items = jnp.searchsorted(jnp.cumsum(sizes), jnp.arange(rows * top), side="right").astype(jnp.int32)
    grid = items.reshape(top, rows).T
    grid = grid[jax.random.permutation(jax.random.fold_in(own, 1), rows)]
    offset_by = jax.random.randint(jax.random.fold_in(own, 2), (rows, 1), 0, top)
    return jnp.take_along_axis(grid, (jnp.arange(top)[None, :] + offset_by) % top, axis=1)


def shares(number_of, total, reach, skew, full):
    weights = [(1 << 20) // math.isqrt(rank ** skew) + 1 for rank in range(1, number_of + 1)]
    largest = reach if full else min(reach, max(-(-total // number_of), total * weights[0] // sum(weights)))
    least = 1 if total - largest >= number_of - 1 else 0
    counts, rest = [largest] + [least] * (number_of - 1), total - largest - least * (number_of - 1)
    while rest > 0:
        free = [i for i in range(1, number_of) if counts[i] < largest] or [i for i in range(1, number_of) if counts[i] < reach]
        pool, remaining = sum([weights[i] for i in free]), rest
        for i in free:
            addition = min(reach - counts[i], max(1, remaining * weights[i] // pool), rest)
            counts[i] = counts[i] + addition
            rest = rest - addition
    return np.array(counts)


def centred(stream_key, shape, deviation, reach, shards=(), kind=jnp.bfloat16):
    gain = steps_of(stream_key, shape, shards, -0.22, 0.18) if shards else 1.0
    values = jax.random.normal(stream_key, shape, jnp.float32) * deviation * gain
    return jnp.minimum(jnp.maximum(values, -reach), reach).astype(kind)


def setup_inputs(seed: int = 0) -> dict:
    keys = jax.random.split(jax.random.key(seed), 11)
    mass_per_volume = jnp.clip(jnp.exp(math.log(2.0) - 1.3862944 * jax.random.uniform(keys[0], (NX, NL), jnp.float32) ** steps_of(keys[0], (NX, NL), ((0, 8), (1, 16)), -0.2, 0.2)), 0.5, 2.0)
    fluid_speed_field = centred(keys[1], (3, NX, NL), 0.5, 3.0, ((1, 8), (2, 16)), jnp.float32)
    fluid_thrust_field = jnp.clip(jnp.exp(math.log(2.0) - 1.3862944 * jax.random.uniform(keys[2], (NX, NL), jnp.float32) ** steps_of(keys[2], (NX, NL), ((0, 8), (1, 16)), -0.2, 0.2)), 0.5, 2.0)
    shock_damping_field = jnp.clip(jnp.exp(math.log(2.0) - 3.6888794 * jax.random.uniform(keys[3], (NX, NL), jnp.float32) ** steps_of(keys[3], (NX, NL), ((0, 8), (1, 16)), -0.2, 0.2)), 0.05, 2.0)
    grain_holding_processor_keys = jax.random.split(jax.random.fold_in(keys[4], 1), GRAIN_COUNT_ALL // PART_DEV)
    grain_holding_processor_turns = jax.random.permutation(jax.random.fold_in(keys[4], 3), GRAIN_COUNT_ALL // PART_DEV)
    grain_holding_processor = jax.vmap(lambda own, number: assign_block(jax.random.fold_in(keys[4], 2), own, number, PART_DEV, DEVICES, 1, CAP, 2))(grain_holding_processor_keys, grain_holding_processor_turns).reshape((GRAIN_COUNT_ALL, 1))
    grain_mesh_slot = touch_ends(jax.random.randint(keys[5], (GRAIN_COUNT_ALL,), 0, CX * LINES_DEV), jax.random.fold_in(keys[5], 1), 0, (CX * LINES_DEV) - 1).astype(jnp.int32)
    grain_speed_vector = centred(keys[6], (3, GRAIN_COUNT_ALL), 0.5, 3.0, ((1, 128),), jnp.float32)
    fluid_speed_at_grain = centred(keys[7], (3, GRAIN_COUNT_ALL), 0.5, 3.0, ((1, 128),), jnp.float32)
    thermal_states = jnp.clip(jnp.exp(math.log(2.0) - 1.3862944 * jax.random.uniform(keys[8], (2, GRAIN_COUNT_ALL), jnp.float32) ** steps_of(keys[8], (2, GRAIN_COUNT_ALL), ((1, 128),), -0.2, 0.2)), 0.5, 2.0)
    grain_mass_over_lag = jnp.clip(jnp.exp(math.log(4.0) - 2.0794415 * jax.random.uniform(keys[9], (GRAIN_COUNT_ALL,), jnp.float32) ** steps_of(keys[9], (GRAIN_COUNT_ALL,), ((0, 128),), -0.2, 0.2)), 0.5, 4.0)
    return {"mass_per_volume": mass_per_volume, "fluid_speed_field": fluid_speed_field, "fluid_thrust_field": fluid_thrust_field, "shock_damping_field": shock_damping_field, "grain_holding_processor": grain_holding_processor, "grain_mesh_slot": grain_mesh_slot, "grain_speed_vector": grain_speed_vector, "fluid_speed_at_grain": fluid_speed_at_grain, "thermal_states": thermal_states, "grain_mass_over_lag": grain_mass_over_lag}


band_one = 0.5
band_two = 0.05
rhs_one = 17.0 / 12.0
rhs_two = 101.0 / 150.0
rhs_three = 0.01
gamma_gas = 1.4
adiabatic_exponent = 0.6


def spectral_derivative(source):
    cell_total = source.shape[1]
    wavenumber = 2.0 * jnp.pi * jnp.arange(cell_total // 2 + 1) / cell_total
    numerator = rhs_one * jnp.sin(wavenumber) + rhs_two / 2.0 * jnp.sin(2.0 * wavenumber) + rhs_three / 3.0 * jnp.sin(3.0 * wavenumber)
    denominator = 1.0 + 2.0 * band_one * jnp.cos(wavenumber) + 2.0 * band_two * jnp.cos(2.0 * wavenumber)
    factor = (numerator / denominator)[None, :, None]
    spectrum = jnp.fft.rfft(source, axis=1)
    return jnp.fft.irfft(1j * factor * spectrum, n=cell_total, axis=1).astype(source.dtype)


def line_rate(mass_per_volume, fluid_speed_field, fluid_thrust_field, shock_damping_field):
    dilatation = spectral_derivative(fluid_speed_field[0:1])[0]
    eff_pressure = fluid_thrust_field - shock_damping_field * dilatation
    energy = fluid_thrust_field / (gamma_gas - 1.0) + 0.5 * mass_per_volume * (fluid_speed_field[0] * fluid_speed_field[0] + fluid_speed_field[1] * fluid_speed_field[1] + fluid_speed_field[2] * fluid_speed_field[2])
    momentum = mass_per_volume * fluid_speed_field[0]
    flux = jnp.stack([momentum, momentum * fluid_speed_field[0] + eff_pressure, momentum * fluid_speed_field[1], momentum * fluid_speed_field[2], (energy + eff_pressure) * fluid_speed_field[0]])
    return -spectral_derivative(flux)


def grain_coupling_feedback(grain_speed_vector, fluid_speed_at_grain, thermal_states, grain_mass_over_lag):
    grain_resistance_push = grain_mass_over_lag[None, :] * (fluid_speed_at_grain - grain_speed_vector)
    resistance_power_deposit = jnp.sum(grain_resistance_push * grain_speed_vector, axis=0) + adiabatic_exponent * grain_mass_over_lag * (thermal_states[1] - thermal_states[0])
    return jnp.concatenate([grain_resistance_push, resistance_power_deposit[None, :]], axis=0)


def reference(mass_per_volume, fluid_speed_field, fluid_thrust_field, shock_damping_field, grain_holding_processor, grain_mesh_slot, grain_speed_vector, fluid_speed_at_grain, thermal_states, grain_mass_over_lag):
    def block_rate(block_index, result):
        first_line = (block_index * LINES_DEV).astype(jnp.int32)

        def take_lines(array):
            return lax.dynamic_slice_in_dim(array, first_line, LINES_DEV, axis=array.ndim - 1)

        rate_block = line_rate(take_lines(mass_per_volume), take_lines(fluid_speed_field), take_lines(fluid_thrust_field), take_lines(shock_damping_field))
        return lax.dynamic_update_slice_in_dim(result, rate_block, first_line, axis=2)

    gas_rate = lax.fori_loop(0, N_SLAB, block_rate, jnp.zeros((5, NX, NL), mass_per_volume.dtype))
    piecewise_share = grain_coupling_feedback(grain_speed_vector, fluid_speed_at_grain, thermal_states, grain_mass_over_lag)
    owners = grain_holding_processor[:, 0].astype(jnp.int32)
    places = grain_mesh_slot.astype(jnp.int32)
    grid_first = (owners // N_SLAB) * CX + places // LINES_DEV
    grid_line = (owners % N_SLAB) * LINES_DEV + places % LINES_DEV
    flat_index = grid_first * NL + grid_line
    flat_rate = gas_rate.reshape(5, NX * NL)
    flat_rate = flat_rate.at[1:, flat_index].add(-piecewise_share)
    return flat_rate.reshape(5, NX, NL)
```

```python
import functools

import jax
import jax.numpy as jnp
import numpy as np
from jax import lax
from jax.experimental import pallas as pl
from jax.experimental.pallas import tpu as pltpu
from jax.sharding import PartitionSpec as P

band_one = 0.5
band_two = 0.05
rhs_one = 17.0 / 12.0
rhs_two = 101.0 / 150.0
rhs_three = 0.01
gamma_gas = 1.4
adiabatic_exponent = 0.6
highest = lax.Precision.HIGHEST
f32 = jnp.float32
bf16 = jnp.bfloat16

HALVES = 2
GROUPS = 4
BUCKETS = HALVES * GROUPS
STEP = 4
CHUNK = 4


def operator_tables(cells):
    sums = np.roots([band_two, band_one, 1.0 - 2.0 * band_two]).real
    roots = np.array([(s + np.sqrt(s * s - 4.0)) / 2.0 for s in sums])
    roots = np.where(np.abs(roots) > 1.0, 1.0 / roots, roots)

    def right_side(z):
        return (
            rhs_one / 2.0 * (z - 1.0 / z)
            + rhs_two / 4.0 * (z**2 - z**-2)
            + rhs_three / 6.0 * (z**3 - z**-3)
        )

    weights = []
    for k in range(2):
        z, other = roots[k], roots[1 - k]
        slope = band_two * (z - 1.0 / z) * (z - other) * (z - 1.0 / other) / z
        weights.append(-right_side(z) / slope)
    direct = rhs_three / 6.0 / band_two
    offsets = np.arange(cells)[None, :] - np.arange(cells)[:, None]
    sizes = np.abs(offsets)
    matrix = sum(w * z**sizes for w, z in zip(weights, roots))
    matrix = np.sign(offsets) * (matrix + direct * (sizes == 1))
    edges = np.zeros((16, cells))
    place = np.arange(cells)
    low = np.zeros((cells, 8))
    high = np.zeros((cells, 8))
    for k in range(2):
        edges[k] = roots[k] ** (cells - 1 - place)
        edges[3 + k] = roots[k] ** place
        low[:, k] = -weights[k] * roots[k] ** (place + 1)
        high[:, 3 + k] = weights[k] * roots[k] ** (cells - place)
    edges[2, cells - 1] = 1.0
    edges[5, 0] = 1.0
    low[0, 2] = -direct
    high[cells - 1, 5] = direct
    full = np.concatenate([matrix, edges]).astype(np.float32)
    return full, edges[:8].astype(np.float32), low.astype(np.float32), high.astype(np.float32)


def halves_of(x):
    top = x.astype(bf16)
    return top, (x - top.astype(f32)).astype(bf16)


def dot_nn(a, b):
    return jnp.dot(a, b, preferred_element_type=f32)


def dot_nt(a, b):
    return lax.dot_general(a, b, (((1,), (1,)), ((), ())), preferred_element_type=f32)


def flux_kernel(
    rho_ref, vel_ref, thrust_ref, damp_ref, left_ref, right_ref, top_ref, rest_ref, low_ref, high_ref,
    rate_ref, edge_ref,
):
    cells = rho_ref.shape[0]
    u, v, w = vel_ref[0], vel_ref[1], vel_ref[2]
    u_top, u_rest = halves_of(u)
    top, rest = top_ref[:cells], rest_ref[:cells]
    dilatation = dot_nn(top, u_top) + dot_nn(rest, u_top) + dot_nn(top, u_rest)
    dilatation = dilatation + jnp.dot(low_ref[...], left_ref[...], precision=highest)
    dilatation = dilatation + jnp.dot(high_ref[...], right_ref[...], precision=highest)
    rho, thrust = rho_ref[...], thrust_ref[...]
    pressure = thrust - damp_ref[...] * dilatation
    energy = thrust / (gamma_gas - 1.0) + 0.5 * rho * (u * u + v * v + w * w)
    momentum = rho * u
    fluxes = [
        momentum,
        momentum * u + pressure,
        momentum * v,
        momentum * w,
        (energy + pressure) * u,
    ]
    for group in ((0, 1), (2, 3), (4,)):
        field = jnp.concatenate([fluxes[c] for c in group], axis=1)
        f_top, f_rest = halves_of(field)
        done = dot_nn(top_ref[...], f_top) + dot_nn(rest_ref[...], f_top) + dot_nn(top_ref[...], f_rest)
        for n, c in enumerate(group):
            rate_ref[c] = -done[:cells, n * 128 : (n + 1) * 128]
            edge_ref[c] = done[cells : cells + 8, n * 128 : (n + 1) * 128]


def bucket_of(cell):
    return (cell >> 15) * GROUPS + ((cell & 127) >> 5)


def fill_kernel(
    peer_ref, peers_ref, cell_ref, cells_ref, speed_ref, fluid_ref, thermal_ref, mass_ref,
    out_ref, top_ref, rest_ref, key_ref, hot_ref, count_ref, rank_ref, total_ref,
):
    peers = out_ref.shape[0] // 10
    blocks = peers_ref.shape[0]
    mass = mass_ref[...]
    work = adiabatic_exponent * mass * (thermal_ref[1:2, :] - thermal_ref[0:1, :])
    rows = []
    for c in range(3):
        speed = speed_ref[c : c + 1, :]
        force = mass * (fluid_ref[c : c + 1, :] - speed)
        work = work + force * speed
        rows.append(force)
    rows.append(work)
    rows.append((cell_ref[...] + 1).astype(f32))
    for c in range(5):
        top = rows[c].astype(bf16).astype(f32)
        top_ref[c : c + 1, :] = top
        rest_ref[c : c + 1, :] = rows[c] - top

    keys = (peers_ref[...] * BUCKETS + bucket_of(cells_ref[...])).astype(f32)
    key_ref[...] = keys
    turned = jnp.concatenate([keys, keys], axis=0).T
    peer_ids = lax.broadcasted_iota(jnp.int32, (peers, 128), 0).astype(bf16)
    bucket_ids = lax.broadcasted_iota(jnp.int32, (BUCKETS, 128), 0)
    earlier = lax.broadcasted_iota(jnp.int32, (128, 128), 0) < lax.broadcasted_iota(jnp.int32, (128, 128), 1)
    slot_ids = lax.broadcasted_iota(jnp.int32, (256, 128), 0).astype(bf16)
    zero = jnp.zeros((), bf16)
    one = jnp.ones((), bf16)

    def buckets_at(i):
        return bucket_of(cells_ref[pl.ds(i, 1), :]) == bucket_ids

    def count_step(t, carry):
        for k in range(CHUNK):
            i = t * CHUNK + k
            peer = peers_ref[pl.ds(i, 1), :].astype(f32).astype(bf16)
            hot = jnp.where(peer_ids == peer, one, zero)
            hot_ref[i] = hot
            mine = jnp.where(buckets_at(i), 1.0, 0.0).astype(bf16)
            count_ref[i] = dot_nt(mine, hot)
        return carry

    lax.fori_loop(0, blocks // CHUNK, count_step, 0)

    def base_step(i, before):
        now = count_ref[i]
        count_ref[i] = before
        return before + now

    counts = lax.fori_loop(0, blocks, base_step, jnp.zeros((BUCKETS, 128), f32))
    starts = [jnp.zeros((1, 128), f32)]
    for b in range(BUCKETS - 1):
        starts.append(starts[-1] + counts[b : b + 1, :])
    start = jnp.concatenate(starts, axis=0)

    def rank_step(t, rolled):
        for k in range(CHUNK):
            i = t * CHUNK + k
            same = (rolled[:, k : k + 1] == key_ref[pl.ds(i, 1), :]) & earlier
            inside = jnp.sum(jnp.where(same, 1.0, 0.0), axis=0, keepdims=True)
            base = dot_nn((count_ref[i] + start).astype(bf16), hot_ref[i])
            base = jnp.sum(jnp.where(buckets_at(i), base, 0.0), axis=0, keepdims=True)
            rank_ref[pl.ds(i, 1), :] = base + inside
        return pltpu.roll(rolled, 128 - CHUNK, 1)

    lax.fori_loop(0, blocks // CHUNK, rank_step, turned)

    total_ref[...] = jnp.zeros_like(total_ref)

    def place_step(t, carry):
        ranks, tops, rests = [], [], []
        for k in range(CHUNK):
            i = t * CHUNK + k
            here = pl.ds(pl.multiple_of(i * 128, 128), 128)
            rank = rank_ref[pl.ds(i, 1), :].astype(bf16)
            ranks.append(jnp.where(slot_ids == rank, one, zero))
            hot = hot_ref[i] != zero
            tops.append(
                jnp.concatenate(
                    [jnp.where(hot, top_ref[c : c + 1, here].astype(bf16), zero) for c in range(5)], axis=0
                )
            )
            rests.append(
                jnp.concatenate(
                    [jnp.where(hot, rest_ref[c : c + 1, here].astype(bf16), zero) for c in range(5)], axis=0
                )
            )
        ranks = jnp.concatenate(ranks, axis=1)
        total_ref[...] += dot_nt(jnp.concatenate(tops, axis=1), ranks) + dot_nt(
            jnp.concatenate(rests, axis=1), ranks
        )
        return carry

    lax.fori_loop(0, blocks // CHUNK, place_step, 0)
    for c in range(5):
        for h in range(2):
            out_ref[pl.ds(2 * c + h, peers, stride=10), :] = total_ref[
                c * peers : (c + 1) * peers, h * 128 : (h + 1) * 128
            ]


def bin_kernel(
    box_ref, rate_ref, left_ref, right_ref, low_ref, high_ref,
    out_ref, x_ref, l_ref, top_ref, rest_ref, total_ref,
):
    span = out_ref.shape[1] // HALVES
    lines = out_ref.shape[2] // GROUPS
    cells = []
    for h in range(2):
        here = slice(h * 128, (h + 1) * 128)
        for c in range(4):
            value = box_ref[pl.ds(2 * c + h, 128, stride=10), :].T
            top = value.astype(bf16).astype(f32)
            top_ref[c, here] = top
            rest_ref[c, here] = value - top
        cell = box_ref[pl.ds(8 + h, 128, stride=10), :].T.astype(jnp.int32) - 1
        x_ref[here] = (cell >> 7).astype(f32)
        l_ref[here] = (cell & 127).astype(f32)
        cells.append(cell)
    cell = jnp.concatenate(cells, axis=0)
    bucket = jnp.where(cell < 0, BUCKETS, bucket_of(cell))
    slot = lax.broadcasted_iota(jnp.int32, cell.shape, 0)
    total_ref[...] = jnp.zeros_like(total_ref)
    x_ids = lax.broadcasted_iota(jnp.int32, (span, 128), 0).astype(bf16)
    l_ids = lax.broadcasted_iota(jnp.int32, (lines, 128), 0).astype(bf16)
    zero = jnp.zeros((), bf16)
    one = jnp.ones((), bf16)
    for b in range(BUCKETS):
        half, group = b // GROUPS, b % GROUPS
        mine = bucket == b
        first = jnp.min(jnp.where(mine, slot, cell.shape[0]))
        last = jnp.max(jnp.where(mine, slot + STEP, 0))

        def step(t, carry, half=half, group=group, b=b):
            xs, tops, rests = [], [], []
            for k in range(STEP):
                row = pl.ds(t * STEP + k, 1)
                x = (x_ref[row, :] - float(half * span)).astype(bf16)
                xs.append(jnp.where(x_ids == x, one, zero))
                hot = l_ids == (l_ref[row, :] - float(group * lines)).astype(bf16)
                tops.append(
                    jnp.concatenate(
                        [jnp.where(hot, top_ref[c, row, :].astype(bf16), zero) for c in range(4)], axis=0
                    )
                )
                rests.append(
                    jnp.concatenate(
                        [jnp.where(hot, rest_ref[c, row, :].astype(bf16), zero) for c in range(4)], axis=0
                    )
                )
            xs = jnp.concatenate(xs, axis=1)
            total_ref[b] += dot_nt(jnp.concatenate(tops, axis=1), xs) + dot_nt(
                jnp.concatenate(rests, axis=1), xs
            )
            return carry

        lax.fori_loop(first // STEP, last // STEP, step, 0)
    for c in range(5):
        rate = rate_ref[c] - jnp.dot(low_ref[...], left_ref[c], precision=highest)
        rate = rate - jnp.dot(high_ref[...], right_ref[c], precision=highest)
        if c == 0:
            out_ref[c] = rate
            continue
        for half in range(HALVES):
            parts = [
                total_ref[half * GROUPS + g, (c - 1) * lines : c * lines, :] for g in range(GROUPS)
            ]
            deposit = jnp.concatenate(parts, axis=0).T
            here = slice(half * span, (half + 1) * span)
            out_ref[c, here] = rate[here] - deposit


def along(block, distance):
    count = lax.axis_size("line")
    return lax.ppermute(block, "line", [(i, (i + distance) % count) for i in range(count)])


def body(
    mass_per_volume,
    fluid_speed_field,
    fluid_thrust_field,
    shock_damping_field,
    grain_holding_processor,
    grain_mesh_slot,
    grain_speed_vector,
    fluid_speed_at_grain,
    thermal_states,
    grain_mass_over_lag,
):
    cells, lines = mass_per_volume.shape
    parts = grain_mesh_slot.shape[0]
    peers = lax.axis_size(("line", "slab"))
    full, edges, low, high = operator_tables(cells)
    full_top = full.astype(jnp.bfloat16)
    full_rest = (full - full_top.astype(np.float32)).astype(jnp.bfloat16)

    edge = jnp.dot(edges, fluid_speed_field[0], precision=highest)
    left, right = along(edge, 1), along(edge, -1)

    blocks = parts // 128
    outgoing = pl.pallas_call(
        fill_kernel,
        name="fill",
        out_shape=jax.ShapeDtypeStruct((peers * 10, 128), f32),
        scratch_shapes=[
            pltpu.VMEM((8, parts), f32),
            pltpu.VMEM((8, parts), f32),
            pltpu.VMEM((blocks, 128), f32),
            pltpu.VMEM((blocks, peers, 128), bf16),
            pltpu.VMEM((blocks, BUCKETS, peers), f32),
            pltpu.VMEM((blocks, 128), f32),
            pltpu.VMEM((5 * peers, 256), f32),
        ],
    )(
        grain_holding_processor.reshape(1, parts),
        grain_holding_processor.reshape(blocks, 128),
        grain_mesh_slot.reshape(1, parts),
        grain_mesh_slot.reshape(blocks, 128),
        grain_speed_vector,
        fluid_speed_at_grain,
        thermal_states,
        grain_mass_over_lag.reshape(1, parts),
    )
    arrived = lax.all_to_all(
        outgoing.reshape(peers, 5, 2, 128), ("line", "slab"), split_axis=0, concat_axis=0, tiled=True
    ).reshape(peers * 10, 128)

    rate, flux_edge = pl.pallas_call(
        flux_kernel,
        name="flux",
        out_shape=(
            jax.ShapeDtypeStruct((5, cells, lines), f32),
            jax.ShapeDtypeStruct((5, 8, lines), f32),
        ),
        cost_estimate=pl.CostEstimate(flops=4 * 10**9, bytes_accessed=4 * 10**6, transcendentals=0),
    )(
        mass_per_volume, fluid_speed_field, fluid_thrust_field, shock_damping_field,
        left, right, full_top, full_rest, low, high,
    )
    flux_left, flux_right = along(flux_edge, 1), along(flux_edge, -1)

    return pl.pallas_call(
        bin_kernel,
        name="bin",
        out_shape=jax.ShapeDtypeStruct((5, cells, lines), f32),
        scratch_shapes=[
            pltpu.VMEM((256, 128), f32),
            pltpu.VMEM((256, 128), f32),
            pltpu.VMEM((4, 256, 128), f32),
            pltpu.VMEM((4, 256, 128), f32),
            pltpu.VMEM((BUCKETS, 4 * lines // GROUPS, cells // HALVES), f32),
        ],
    )(arrived, rate, flux_left, flux_right, low, high)


def solution(mesh):
    placed = (
        P("line", "slab"),
        P(None, "line", "slab"),
        P("line", "slab"),
        P("line", "slab"),
        P(("line", "slab"), None),
        P(("line", "slab")),
        P(None, ("line", "slab")),
        P(None, ("line", "slab")),
        P(None, ("line", "slab")),
        P(("line", "slab")),
    )
    return jax.shard_map(
        body, mesh=mesh, in_specs=placed, out_specs=P(None, "line", "slab"), check_vma=False
    )
```

```python
import jax
import jax.numpy as jnp
import numpy as np
from jax import lax
from jax.experimental import pallas as pl
from jax.experimental.pallas import tpu as pltpu
from jax.sharding import PartitionSpec as P


band_one = 0.5
band_two = 0.05
rhs_one = 17.0 / 12.0
rhs_two = 101.0 / 150.0
rhs_three = 0.01
gamma_gas = 1.4
adiabatic_exponent = 0.6
highest = lax.Precision.HIGHEST
f32 = jnp.float32
bf16 = jnp.bfloat16

HALVES = 2
GROUPS = 4
BUCKETS = HALVES * GROUPS
STEP = 8
PAIR = 4
CHUNK = 16


def operator_tables(cells):
    sums = np.roots([band_two, band_one, 1.0 - 2.0 * band_two]).real
    roots = np.array([(s + np.sqrt(s * s - 4.0)) / 2.0 for s in sums])
    roots = np.where(np.abs(roots) > 1.0, 1.0 / roots, roots)

    def right_side(z):
        return (
            rhs_one / 2.0 * (z - 1.0 / z)
            + rhs_two / 4.0 * (z**2 - z**-2)
            + rhs_three / 6.0 * (z**3 - z**-3)
        )

    weights = []
    for k in range(2):
        z, other = roots[k], roots[1 - k]
        slope = band_two * (z - 1.0 / z) * (z - other) * (z - 1.0 / other) / z
        weights.append(-right_side(z) / slope)
    direct = rhs_three / 6.0 / band_two
    offsets = np.arange(cells)[None, :] - np.arange(cells)[:, None]
    sizes = np.abs(offsets)
    matrix = sum(w * z**sizes for w, z in zip(weights, roots))
    matrix = np.sign(offsets) * (matrix + direct * (sizes == 1))
    edges = np.zeros((16, cells))
    place = np.arange(cells)
    low = np.zeros((cells, 8))
    high = np.zeros((cells, 8))
    for k in range(2):
        edges[k] = roots[k] ** (cells - 1 - place)
        edges[3 + k] = roots[k] ** place
        low[:, k] = -weights[k] * roots[k] ** (place + 1)
        high[:, 3 + k] = weights[k] * roots[k] ** (cells - place)
    edges[2, cells - 1] = 1.0
    edges[5, 0] = 1.0
    low[0, 2] = -direct
    high[cells - 1, 5] = direct
    full = np.concatenate([matrix, edges]).astype(np.float32)
    return full, edges[:8].astype(np.float32), low.astype(np.float32), high.astype(np.float32)


def halves_of(x):
    top = x.astype(bf16)
    return top, (x - top.astype(f32)).astype(bf16)


def dot_nn(a, b):
    return jnp.dot(a, b, preferred_element_type=f32)


def dot_nt(a, b):
    return lax.dot_general(a, b, (((1,), (1,)), ((), ())), preferred_element_type=f32)


def flux_kernel(
    rho_ref, vel_ref, thrust_ref, damp_ref, left_ref, right_ref, full_ref, fix_ref,
    rate_ref, edge_ref,
):
    cells = rho_ref.shape[0]
    u, v, w = vel_ref[0], vel_ref[1], vel_ref[2]
    u_top, u_rest = halves_of(u)
    dilatation = dot_nn(full_ref[:cells], jnp.concatenate([u_top, u_top, u_rest], axis=0))
    sent_top, sent_rest = halves_of(jnp.concatenate([left_ref[...], right_ref[...]], axis=0))
    dilatation = dilatation + dot_nn(
        fix_ref[...], jnp.concatenate([sent_top, sent_top, sent_rest], axis=0)
    )
    rho, thrust = rho_ref[...], thrust_ref[...]
    pressure = thrust - damp_ref[...] * dilatation
    energy = thrust / (gamma_gas - 1.0) + 0.5 * rho * (u * u + v * v + w * w)
    momentum = rho * u
    fluxes = [
        momentum,
        momentum * u + pressure,
        momentum * v,
        momentum * w,
        (energy + pressure) * u,
    ]
    for group in ((0, 1), (2, 3), (4,)):
        field = jnp.concatenate([fluxes[c] for c in group], axis=1)
        f_top, f_rest = halves_of(field)
        done = dot_nn(full_ref[...], jnp.concatenate([f_top, f_top, f_rest], axis=0))
        for n, c in enumerate(group):
            rate_ref[c] = -done[:cells, n * 128 : (n + 1) * 128]
            edge_ref[c] = done[cells : cells + 8, n * 128 : (n + 1) * 128]


def spread(block, k, copies):
    wide = jnp.broadcast_to(block[k : k + 1, :], (16, 128)).astype(bf16)
    return jnp.concatenate([wide] * copies, axis=0)


def bucket_of(cell):
    return (cell >> 15) * GROUPS + ((cell & 127) >> 5)


def fill_kernel(
    peer_ref, peers_ref, cell_ref, cells_ref, speed_ref, fluid_ref, thermal_ref, mass_ref,
    out_ref, top_ref, rest_ref, key_ref, hot_ref, count_ref, total_ref,
):
    peers = out_ref.shape[0] // 10
    blocks = peers_ref.shape[0]
    mass = mass_ref[...]
    work = adiabatic_exponent * mass * (thermal_ref[1:2, :] - thermal_ref[0:1, :])
    rows = []
    for c in range(3):
        speed = speed_ref[c : c + 1, :]
        force = mass * (fluid_ref[c : c + 1, :] - speed)
        work = work + force * speed
        rows.append(force)
    rows.append(work)
    rows.append((cell_ref[...] + 1).astype(f32))
    for c in range(5):
        top = rows[c].astype(bf16).astype(f32)
        top_ref[c : c + 1, :] = top
        rest_ref[c : c + 1, :] = rows[c] - top

    keys = (peers_ref[...] * BUCKETS + bucket_of(cells_ref[...])).astype(f32)
    key_ref[...] = keys
    turned = jnp.concatenate([keys, keys], axis=0).T
    peer_ids = lax.broadcasted_iota(jnp.int32, (peers, 128), 0).astype(bf16)
    bucket_ids = lax.broadcasted_iota(jnp.int32, (BUCKETS, 128), 0)
    earlier = lax.broadcasted_iota(jnp.int32, (128, 128), 0) < lax.broadcasted_iota(jnp.int32, (128, 128), 1)
    slot_ids = lax.broadcasted_iota(jnp.int32, (256, 128), 0).astype(bf16)
    zero = jnp.zeros((), bf16)
    one = jnp.ones((), bf16)

    def buckets_at(block, k):
        return block[k : k + 1, :] == bucket_ids

    def count_step(t, carry):
        for n in range(2):
            rows = pl.ds(pl.multiple_of((2 * t + n) * CHUNK, CHUNK), CHUNK)
            peer_rows = peers_ref[rows, :].astype(f32)
            bucket_rows = bucket_of(cells_ref[rows, :])
            for k in range(CHUNK):
                i = (2 * t + n) * CHUNK + k
                hot = jnp.where(peer_ids == spread(peer_rows, k, peers // 16), one, zero)
                hot_ref[i] = hot
                mine = jnp.where(buckets_at(bucket_rows, k), 1.0, 0.0).astype(bf16)
                count_ref[i] = dot_nt(mine, hot)
        return carry

    lax.fori_loop(0, blocks // (2 * CHUNK), count_step, 0)

    def base_step(t, before):
        for k in range(CHUNK):
            now = count_ref[t * CHUNK + k]
            count_ref[t * CHUNK + k] = before
            before = before + now
        return before

    counts = lax.fori_loop(0, blocks // CHUNK, base_step, jnp.zeros((BUCKETS, 128), f32))
    room = [None] * BUCKETS
    left = jnp.full((1, 128), 256.0)
    for b in reversed(range(BUCKETS)):
        left = left - counts[b : b + 1, :]
        room[b] = left
    starts = []
    end = jnp.zeros((1, 128), f32)
    for b in range(BUCKETS):
        starts.append(jnp.minimum(jnp.maximum(end, float(b * 256 // BUCKETS)), room[b]))
        end = starts[-1] + counts[b : b + 1, :]
    start = jnp.concatenate(starts, axis=0)

    rounds = blocks // CHUNK

    def rank_rows(t, rolled):
        rows = pl.ds(pl.multiple_of(t * CHUNK, CHUNK), CHUNK)
        key_rows = key_ref[rows, :]
        bucket_rows = bucket_of(cells_ref[rows, :])
        ranks = []
        for k in range(CHUNK):
            i = t * CHUNK + k
            same = (rolled[:, k : k + 1] == key_rows[k : k + 1, :]) & earlier
            inside = jnp.sum(jnp.where(same, 1.0, 0.0), axis=0, keepdims=True)
            base = dot_nn((count_ref[i] + start).astype(bf16), hot_ref[i])
            base = jnp.sum(jnp.where(buckets_at(bucket_rows, k), base, 0.0), axis=0, keepdims=True)
            ranks.append(base + inside)
        return jnp.concatenate(ranks, axis=0), pltpu.roll(rolled, 128 - CHUNK, 1)

    total_ref[...] = jnp.zeros_like(total_ref)

    def place_step(t, carry):
        rank_rows_now, rolled = carry
        rows = pl.ds(pl.multiple_of(t * CHUNK, CHUNK), CHUNK)
        peer_rows = peers_ref[rows, :].astype(f32)
        sums = None
        for pair in range(CHUNK // PAIR):
            ranks, values = [], []
            for k in range(pair * PAIR, (pair + 1) * PAIR):
                here = pl.ds(pl.multiple_of((t * CHUNK + k) * 128, 128), 128)
                ranks.append(jnp.where(slot_ids == spread(rank_rows_now, k, 16), one, zero))
                hot = peer_ids == spread(peer_rows, k, peers // 16)
                top_rows, rest_rows = top_ref[:, here], rest_ref[:, here]
                parts = [jnp.where(hot, spread(top_rows, c, peers // 16), zero) for c in range(5)]
                parts += [jnp.where(hot, spread(rest_rows, c, peers // 16), zero) for c in range(5)]
                values.append(jnp.concatenate(parts, axis=0))
            ranks = jnp.concatenate(ranks, axis=1)
            part = dot_nt(jnp.concatenate(values, axis=1), ranks)
            sums = part if sums is None else sums + part
        following = rank_rows(jnp.minimum(t + 1, rounds - 1), rolled)
        total_ref[...] += sums
        return following

    lax.fori_loop(0, rounds, place_step, rank_rows(0, turned))
    for c in range(5):
        for h in range(2):
            here = slice(h * 128, (h + 1) * 128)
            out_ref[pl.ds(2 * c + h, peers, stride=10), :] = (
                total_ref[c * peers : (c + 1) * peers, here]
                + total_ref[(c + 5) * peers : (c + 6) * peers, here]
            )


def bin_kernel(
    box_ref, rate_ref, left_ref, right_ref, fix_ref,
    out_ref, x_ref, l_ref, value_ref, total_ref,
):
    span = out_ref.shape[1] // HALVES
    lines = out_ref.shape[2] // GROUPS
    slots = 256
    lows, highs = [], []
    for h in range(2):
        here = slice(h * 128, (h + 1) * 128)
        for c in range(4):
            value = box_ref[pl.ds(2 * c + h, 128, stride=10), :].T
            top = value.astype(bf16).astype(f32)
            value_ref[c, here] = top
            value_ref[4 + c, here] = value - top
        arrived = box_ref[pl.ds(8 + h, 128, stride=10), :]
        cell = arrived.T.astype(jnp.int32) - 1
        across = (cell >> 7).astype(f32)
        for half in range(HALVES):
            x_ref[half, here] = across - float(half * span)
        l_ref[here] = (cell & 127).astype(f32)
        cell = arrived.astype(jnp.int32) - 1
        bucket = jnp.where(cell < 0, BUCKETS, bucket_of(cell))
        slot = lax.broadcasted_iota(jnp.int32, (1, 128), 1).astype(f32) + float(h * 128)
        found = [
            jnp.max(jnp.where(bucket == b, 1.0, 0.0), axis=0, keepdims=True) for b in range(BUCKETS)
        ]
        found = jnp.concatenate(found, axis=0) > 0.0
        lows.append(jnp.where(found, slot, float(slots)))
        highs.append(jnp.where(found, slot + 1.0, 0.0))
    x_ref[:, slots:] = jnp.full((HALVES, x_ref.shape[1] - slots, 128), -512.0)
    l_ref[slots:] = jnp.zeros((l_ref.shape[0] - slots, 128), f32)
    value_ref[:, slots:] = jnp.zeros((8, value_ref.shape[1] - slots, 128), f32)
    low = jnp.min(jnp.minimum(lows[0], lows[1]), axis=1, keepdims=True)
    high = jnp.max(jnp.maximum(highs[0], highs[1]), axis=1, keepdims=True)
    low = (low.astype(jnp.int32) // STEP) * STEP
    rounds = (jnp.max(high.astype(jnp.int32) - low) + (STEP - 1)) // STEP
    firsts = [jnp.max(low[b : b + 1, :]) for b in range(BUCKETS)]
    total_ref[...] = jnp.zeros_like(total_ref)
    x_ids = lax.broadcasted_iota(jnp.int32, (span, 128), 0).astype(bf16)
    l_ids = [
        (lax.broadcasted_iota(jnp.int32, (lines, 128), 0) + g * lines).astype(bf16) for g in range(GROUPS)
    ]
    zero = jnp.zeros((), bf16)
    one = jnp.ones((), bf16)

    def step(t, carry):
        for b in range(BUCKETS):
            half, group = b // GROUPS, b % GROUPS
            first = pl.multiple_of(jnp.minimum(firsts[b] + t * STEP, slots), STEP)
            rows = pl.ds(first, STEP)
            x_rows, l_rows = x_ref[half, rows, :], l_ref[rows, :]
            value_rows = [value_ref[c, rows, :] for c in range(8)]
            sums = None
            for pair in range(STEP // PAIR):
                xs, values = [], []
                for k in range(pair * PAIR, (pair + 1) * PAIR):
                    xs.append(jnp.where(x_ids == spread(x_rows, k, span // 16), one, zero))
                    hot = l_ids[group] == spread(l_rows, k, lines // 16)
                    parts = [
                        jnp.where(hot, spread(value_rows[c], k, lines // 16), zero) for c in range(8)
                    ]
                    values.append(jnp.concatenate(parts, axis=0))
                xs = jnp.concatenate(xs, axis=1)
                part = dot_nt(jnp.concatenate(values, axis=1), xs)
                sums = part if sums is None else sums + part
            total_ref[b] += sums
        return carry

    lax.fori_loop(0, rounds, step, 0)
    sent = jnp.concatenate(
        [jnp.concatenate([left_ref[c], right_ref[c]], axis=0) for c in range(5)], axis=1
    )
    sent_top, sent_rest = halves_of(sent)
    shift = dot_nn(fix_ref[...], jnp.concatenate([sent_top, sent_top, sent_rest], axis=0))
    for c in range(5):
        rate = rate_ref[c] - shift[:, c * 128 : (c + 1) * 128]
        if c == 0:
            out_ref[c] = rate
            continue
        for half in range(HALVES):
            parts = [
                total_ref[half * GROUPS + g, (c - 1) * lines : c * lines, :]
                + total_ref[half * GROUPS + g, (c + 3) * lines : (c + 4) * lines, :]
                for g in range(GROUPS)
            ]
            deposit = jnp.concatenate(parts, axis=0).T
            here = slice(half * span, (half + 1) * span)
            out_ref[c, here] = rate[here] - deposit


def along(block, distance):
    count = lax.axis_size("line")
    return lax.ppermute(block, "line", [(i, (i + distance) % count) for i in range(count)])


def run_fill(
    peers, grain_holding_processor, grain_mesh_slot, grain_speed_vector, fluid_speed_at_grain,
    thermal_states, grain_mass_over_lag,
):
    parts = grain_mesh_slot.shape[0]
    blocks = parts // 128
    return pl.pallas_call(
        fill_kernel,
        name="fill",
        compiler_params=pltpu.CompilerParams(vmem_limit_bytes=20 << 20),
        out_shape=jax.ShapeDtypeStruct((peers * 10, 128), f32),
        scratch_shapes=[
            pltpu.VMEM((8, parts), f32),
            pltpu.VMEM((8, parts), f32),
            pltpu.VMEM((blocks, 128), f32),
            pltpu.VMEM((blocks, peers, 128), bf16),
            pltpu.VMEM((blocks, BUCKETS, peers), f32),
            pltpu.VMEM((10 * peers, 256), f32),
        ],
    )(
        grain_holding_processor.reshape(1, parts),
        grain_holding_processor.reshape(blocks, 128),
        grain_mesh_slot.reshape(1, parts),
        grain_mesh_slot.reshape(blocks, 128),
        grain_speed_vector,
        fluid_speed_at_grain,
        thermal_states,
        grain_mass_over_lag.reshape(1, parts),
    )


def run_bin(arrived, rate, flux_left, flux_right, fix):
    cells, lines = rate.shape[1:]
    return pl.pallas_call(
        bin_kernel,
        name="bin",
        compiler_params=pltpu.CompilerParams(vmem_limit_bytes=20 << 20),
        out_shape=jax.ShapeDtypeStruct((5, cells, lines), f32),
        scratch_shapes=[
            pltpu.VMEM((HALVES, 256 + 2 * STEP, 128), f32),
            pltpu.VMEM((256 + 2 * STEP, 128), f32),
            pltpu.VMEM((8, 256 + 2 * STEP, 128), f32),
            pltpu.VMEM((BUCKETS, 8 * lines // GROUPS, cells // HALVES), f32),
        ],
    )(arrived, rate, flux_left, flux_right, fix)


def body(
    mass_per_volume,
    fluid_speed_field,
    fluid_thrust_field,
    shock_damping_field,
    grain_holding_processor,
    grain_mesh_slot,
    grain_speed_vector,
    fluid_speed_at_grain,
    thermal_states,
    grain_mass_over_lag,
):
    cells, lines = mass_per_volume.shape
    peers = lax.axis_size(("line", "slab"))
    full, edges, low, high = operator_tables(cells)
    full_top = full.astype(jnp.bfloat16)
    full_rest = (full - full_top.astype(np.float32)).astype(jnp.bfloat16)
    full = np.concatenate([full_top, full_rest, full_top], axis=1)
    fix = np.concatenate([low, high], axis=1)
    fix_top = fix.astype(jnp.bfloat16)
    fix_rest = (fix - fix_top.astype(np.float32)).astype(jnp.bfloat16)
    fix = np.concatenate([fix_top, fix_rest, fix_top], axis=1)

    edge = jnp.dot(edges, fluid_speed_field[0], precision=highest)
    left = along(edge, 1)
    right = along(edge, -1)
    outgoing = run_fill(
        peers, grain_holding_processor, grain_mesh_slot, grain_speed_vector, fluid_speed_at_grain,
        thermal_states, grain_mass_over_lag,
    )
    arrived = lax.all_to_all(
        outgoing.reshape(peers, 5, 2, 128), ("line", "slab"), split_axis=0, concat_axis=0, tiled=True
    ).reshape(peers * 10, 128)

    rate, flux_edge = pl.pallas_call(
        flux_kernel,
        name="flux",
        compiler_params=pltpu.CompilerParams(vmem_limit_bytes=20 << 20),
        out_shape=(
            jax.ShapeDtypeStruct((5, cells, lines), f32),
            jax.ShapeDtypeStruct((5, 8, lines), f32),
        ),
        cost_estimate=pl.CostEstimate(flops=4 * 10**9, bytes_accessed=4 * 10**6, transcendentals=0),
    )(
        mass_per_volume, fluid_speed_field, fluid_thrust_field, shock_damping_field,
        left, right, full, fix,
    )
    flux_left, flux_right = along(flux_edge, 1), along(flux_edge, -1)

    return run_bin(arrived, rate, flux_left, flux_right, fix)


def solution(mesh):
    placed = (
        P("line", "slab"),
        P(None, "line", "slab"),
        P("line", "slab"),
        P("line", "slab"),
        P(("line", "slab"), None),
        P(("line", "slab")),
        P(None, ("line", "slab")),
        P(None, ("line", "slab")),
        P(None, ("line", "slab")),
        P(("line", "slab")),
    )
    return jax.shard_map(
        body, mesh=mesh, in_specs=placed, out_specs=P(None, "line", "slab"), check_vma=False
    )
```

```python
import functools

import jax
import jax.numpy as jnp
import numpy as np
from jax import lax
from jax.experimental import pallas as pl
from jax.experimental.pallas import tpu as pltpu
from jax.sharding import PartitionSpec as P

band_one = 0.5
band_two = 0.05
rhs_one = 17.0 / 12.0
rhs_two = 101.0 / 150.0
rhs_three = 0.01
gamma_gas = 1.4
adiabatic_exponent = 0.6
highest = lax.Precision.HIGHEST
f32 = jnp.float32
bf16 = jnp.bfloat16

HALVES = 2
GROUPS = 4
BUCKETS = HALVES * GROUPS
STEP = 8
PAIR = 4
CHUNK = 16


def stacked_of(table):
    table = table.astype(np.float32)
    top = table.astype(jnp.bfloat16)
    rest = (table - top.astype(np.float32)).astype(jnp.bfloat16)
    return np.concatenate([top, rest, top], axis=1)


def operator_tables(cells):
    sums = np.roots([band_two, band_one, 1.0 - 2.0 * band_two]).real
    roots = np.array([(s + np.sqrt(s * s - 4.0)) / 2.0 for s in sums])
    roots = np.where(np.abs(roots) > 1.0, 1.0 / roots, roots)

    def right_side(z):
        return (
            rhs_one / 2.0 * (z - 1.0 / z)
            + rhs_two / 4.0 * (z**2 - z**-2)
            + rhs_three / 6.0 * (z**3 - z**-3)
        )

    weights = []
    for k in range(2):
        z, other = roots[k], roots[1 - k]
        slope = band_two * (z - 1.0 / z) * (z - other) * (z - 1.0 / other) / z
        weights.append(-right_side(z) / slope)
    direct = rhs_three / 6.0 / band_two
    place = np.arange(cells)
    reach = cells // 128
    blocks = []
    for apart in range(1 - reach, reach):
        offsets = 128 * apart + place[None, :128] - place[:128, None]
        sizes = np.abs(offsets)
        block = sum(w * z**sizes for w, z in zip(weights, roots))
        blocks.append(np.sign(offsets) * (block + direct * (sizes == 1)))
    blocks = np.concatenate(blocks)
    up, down = np.zeros((8, cells)), np.zeros((8, cells))
    low, high = np.zeros((cells, 8)), np.zeros((cells, 8))
    for k in range(2):
        up[k] = roots[k] ** (cells - 1 - place)
        down[k] = roots[k] ** place
        low[:, k] = -weights[k] * roots[k] ** (place + 1)
        high[:, k] = weights[k] * roots[k] ** (cells - place)
    up[2, cells - 1] = 1.0
    down[2, 0] = 1.0
    low[0, 2] = -direct
    high[cells - 1, 2] = direct
    probe = []
    for sums in (up, down):
        mixed = np.zeros((24, cells))
        for m in range(6):
            added = low[:, m] if m < 3 else high[:, m - 3]
            for k in range(3):
                mixed[(m // 2) * 8 + (m % 2) * 4 + k] = sums[k] * added
        probe += [sums, mixed]
    probe = np.concatenate(probe)
    fix = np.concatenate([low, high], axis=1)
    return stacked_of(blocks)[:, :256], stacked_of(probe), stacked_of(fix)


def halves_of(x):
    top = x.astype(bf16)
    return top, (x - top.astype(f32)).astype(bf16)


def dot_nn(a, b):
    return jnp.dot(a, b, preferred_element_type=f32)


def dot_nt(a, b):
    return lax.dot_general(a, b, (((1,), (1,)), ((), ())), preferred_element_type=f32)


def stack_of(x):
    top, rest = halves_of(x)
    return jnp.concatenate([top, top, rest], axis=0)


def operator_of(block_ref, cells):
    reach = cells // 128
    rows = []
    for i in range(reach):
        parts = []
        for part in (0, 1, 0):
            for j in range(reach):
                n = j - i + reach - 1
                parts.append(block_ref[n * 128 : (n + 1) * 128, part * 128 : (part + 1) * 128])
        rows.append(jnp.concatenate(parts, axis=1))
    return jnp.concatenate(rows, axis=0)


def fluxes_of(rho, vel_ref, thrust, damp, dilatation):
    u, v, w = vel_ref[0], vel_ref[1], vel_ref[2]
    pressure = thrust - damp * dilatation
    energy = thrust / (gamma_gas - 1.0) + 0.5 * rho * (u * u + v * v + w * w)
    momentum = rho * u
    return [
        momentum,
        momentum * u + pressure,
        momentum * v,
        momentum * w,
        (energy + pressure) * u,
    ]


def edge_kernel(
    rho_ref, vel_ref, thrust_ref, damp_ref, block_ref, probe_ref,
    own_ref, up_ref, down_ref, far_up_ref, far_down_ref,
):
    cells, lines = rho_ref.shape
    u, damp = vel_ref[0], damp_ref[...]
    own = dot_nn(operator_of(block_ref, cells), stack_of(u))
    own_ref[...] = own
    fields = [u] + fluxes_of(rho_ref[...], vel_ref, thrust_ref[...], damp, own) + [damp, damp * u]
    sums = dot_nn(probe_ref[...], stack_of(jnp.concatenate(fields, axis=1)))
    for first, out_ref, far_ref in ((0, up_ref, far_up_ref), (32, down_ref, far_down_ref)):
        for n in range(6):
            out_ref[n * 8 : (n + 1) * 8] = sums[first : first + 8, n * lines : (n + 1) * lines]
        for n in range(2):
            here = slice((6 + n) * lines, (7 + n) * lines)
            out_ref[48 + n * 24 : 72 + n * 24] = sums[first + 8 : first + 32, here]
        far_ref[...] = sums[first : first + 8, :lines]


def neighbour_sums(near_ref, low, high):
    mix = [low[m : m + 1] for m in range(3)] + [high[m : m + 1] for m in range(3)]
    wide = [jnp.broadcast_to(row, (4, row.shape[1])) for row in mix]
    found = []
    for c in range(5):
        base = near_ref[(1 + c) * 8 : (2 + c) * 8]
        if c in (1, 4):
            first = 48 if c == 1 else 72
            added = sum(
                near_ref[first + q * 8 : first + (q + 1) * 8]
                * jnp.concatenate([wide[2 * q], wide[2 * q + 1]], axis=0)
                for q in range(3)
            )
            base = base - added - pltpu.roll(added, 4, 0)
        found.append(base)
    return jnp.concatenate(found, axis=1)


def flux_kernel(
    rho_ref, vel_ref, thrust_ref, damp_ref, own_ref, up_ref, down_ref,
    left_ref, right_ref, far_left_ref, far_right_ref, block_ref, fix_ref, rate_ref,
):
    cells, lines = rho_ref.shape
    full = operator_of(block_ref, cells)
    near = jnp.concatenate([left_ref[:8], right_ref[:8]], axis=0)
    dilatation = own_ref[...] + dot_nn(fix_ref[...], stack_of(near))
    fluxes = fluxes_of(rho_ref[...], vel_ref, thrust_ref[...], damp_ref[...], dilatation)
    sums = jnp.concatenate(
        [
            neighbour_sums(left_ref, far_left_ref[...], down_ref[:8]),
            neighbour_sums(right_ref, up_ref[:8], far_right_ref[...]),
        ],
        axis=0,
    )
    added = dot_nn(fix_ref[...], stack_of(sums))
    for group in ((0, 1), (2, 3), (4,)):
        field = jnp.concatenate([fluxes[c] for c in group], axis=1)
        done = dot_nn(full, stack_of(field))
        for n, c in enumerate(group):
            rate_ref[c] = -(
                done[:, n * lines : (n + 1) * lines] + added[:, c * lines : (c + 1) * lines]
            )


def spread(block, k, copies):
    wide = jnp.broadcast_to(block[k : k + 1, :], (16, 128)).astype(bf16)
    return jnp.concatenate([wide] * copies, axis=0)


def bucket_of(cell):
    return (cell >> 15) * GROUPS + ((cell & 127) >> 5)


def fill_kernel(
    *refs,
):
    sources, out_ref, targets, sems = refs[:7], refs[7], refs[8:15], refs[15]
    top_ref, rest_ref, key_ref, hot_ref, count_ref, total_ref = refs[16:]
    peers_ref, cells_ref, cell_ref, speed_ref, fluid_ref, thermal_ref, mass_ref = targets
    copies = [
        pltpu.make_async_copy(source, target, sems.at[n])
        for n, (source, target) in enumerate(zip(sources, targets))
    ]
    for copy in copies:
        copy.start()
    for copy in copies:
        copy.wait()
    peers = out_ref.shape[0] // 10
    blocks = peers_ref.shape[0]
    mass = mass_ref[...]
    work = adiabatic_exponent * mass * (thermal_ref[1:2, :] - thermal_ref[0:1, :])
    rows = []
    for c in range(3):
        speed = speed_ref[c : c + 1, :]
        force = mass * (fluid_ref[c : c + 1, :] - speed)
        work = work + force * speed
        rows.append(force)
    rows.append(work)
    rows.append((cell_ref[...] + 1).astype(f32))
    for c in range(5):
        top = rows[c].astype(bf16).astype(f32)
        top_ref[c : c + 1, :] = top
        rest_ref[c : c + 1, :] = rows[c] - top

    keys = (peers_ref[...] * BUCKETS + bucket_of(cells_ref[...])).astype(f32)
    key_ref[...] = keys
    turned = jnp.concatenate([keys, keys], axis=0).T
    peer_ids = lax.broadcasted_iota(jnp.int32, (peers, 128), 0).astype(bf16)
    bucket_ids = lax.broadcasted_iota(jnp.int32, (BUCKETS, 128), 0)
    earlier = lax.broadcasted_iota(jnp.int32, (128, 128), 0) < lax.broadcasted_iota(jnp.int32, (128, 128), 1)
    slot_ids = lax.broadcasted_iota(jnp.int32, (256, 128), 0).astype(bf16)
    zero = jnp.zeros((), bf16)
    one = jnp.ones((), bf16)

    def buckets_at(block, k):
        return block[k : k + 1, :] == bucket_ids

    def count_step(t, carry):
        for n in range(2):
            rows = pl.ds(pl.multiple_of((2 * t + n) * CHUNK, CHUNK), CHUNK)
            peer_rows = peers_ref[rows, :].astype(f32)
            bucket_rows = bucket_of(cells_ref[rows, :])
            for k in range(CHUNK):
                i = (2 * t + n) * CHUNK + k
                hot = jnp.where(peer_ids == spread(peer_rows, k, peers // 16), one, zero)
                hot_ref[i] = hot
                mine = jnp.where(buckets_at(bucket_rows, k), 1.0, 0.0).astype(bf16)
                count_ref[i] = dot_nt(mine, hot)
        return carry

    lax.fori_loop(0, blocks // (2 * CHUNK), count_step, 0)

    def base_step(t, before):
        for k in range(CHUNK):
            now = count_ref[t * CHUNK + k]
            count_ref[t * CHUNK + k] = before
            before = before + now
        return before

    counts = lax.fori_loop(0, blocks // CHUNK, base_step, jnp.zeros((BUCKETS, 128), f32))
    room = [None] * BUCKETS
    left = jnp.full((1, 128), 256.0)
    for b in reversed(range(BUCKETS)):
        left = left - counts[b : b + 1, :]
        room[b] = left
    starts = []
    end = jnp.zeros((1, 128), f32)
    for b in range(BUCKETS):
        starts.append(jnp.minimum(jnp.maximum(end, float(b * 256 // BUCKETS)), room[b]))
        end = starts[-1] + counts[b : b + 1, :]
    start = jnp.concatenate(starts, axis=0)

    rounds = blocks // CHUNK

    def rank_rows(t, rolled):
        rows = pl.ds(pl.multiple_of(t * CHUNK, CHUNK), CHUNK)
        key_rows = key_ref[rows, :]
        bucket_rows = bucket_of(cells_ref[rows, :])
        ranks = []
        for k in range(CHUNK):
            i = t * CHUNK + k
            same = (rolled[:, k : k + 1] == key_rows[k : k + 1, :]) & earlier
            inside = jnp.sum(jnp.where(same, 1.0, 0.0), axis=0, keepdims=True)
            base = dot_nn((count_ref[i] + start).astype(bf16), hot_ref[i])
            base = jnp.sum(jnp.where(buckets_at(bucket_rows, k), base, 0.0), axis=0, keepdims=True)
            ranks.append(base + inside)
        return jnp.concatenate(ranks, axis=0), pltpu.roll(rolled, 128 - CHUNK, 1)

    total_ref[...] = jnp.zeros_like(total_ref)

    def place_step(t, carry):
        rank_rows_now, rolled = carry
        rows = pl.ds(pl.multiple_of(t * CHUNK, CHUNK), CHUNK)
        peer_rows = peers_ref[rows, :].astype(f32)
        sums = None
        for pair in range(CHUNK // PAIR):
            ranks, values = [], []
            for k in range(pair * PAIR, (pair + 1) * PAIR):
                here = pl.ds(pl.multiple_of((t * CHUNK + k) * 128, 128), 128)
                ranks.append(jnp.where(slot_ids == spread(rank_rows_now, k, 16), one, zero))
                hot = peer_ids == spread(peer_rows, k, peers // 16)
                top_rows, rest_rows = top_ref[:, here], rest_ref[:, here]
                parts = [jnp.where(hot, spread(top_rows, c, peers // 16), zero) for c in range(5)]
                parts += [jnp.where(hot, spread(rest_rows, c, peers // 16), zero) for c in range(5)]
                values.append(jnp.concatenate(parts, axis=0))
            ranks = jnp.concatenate(ranks, axis=1)
            part = dot_nt(jnp.concatenate(values, axis=1), ranks)
            sums = part if sums is None else sums + part
        following = rank_rows(jnp.minimum(t + 1, rounds - 1), rolled)
        total_ref[...] += sums
        return following

    lax.fori_loop(0, rounds, place_step, rank_rows(0, turned))
    for c in range(5):
        for h in range(2):
            here = slice(h * 128, (h + 1) * 128)
            out_ref[pl.ds(2 * c + h, peers, stride=10), :] = (
                total_ref[c * peers : (c + 1) * peers, here]
                + total_ref[(c + 5) * peers : (c + 6) * peers, here]
            )


def bin_kernel(
    box_ref, rate_ref, out_ref, x_ref, l_ref, value_ref, total_ref,
):
    span = out_ref.shape[1] // HALVES
    lines = out_ref.shape[2] // GROUPS
    slots = 256
    lows, highs = [], []
    for h in range(2):
        here = slice(h * 128, (h + 1) * 128)
        for c in range(4):
            value = box_ref[pl.ds(2 * c + h, 128, stride=10), :].T
            top = value.astype(bf16).astype(f32)
            value_ref[c, here] = top
            value_ref[4 + c, here] = value - top
        arrived = box_ref[pl.ds(8 + h, 128, stride=10), :]
        cell = arrived.T.astype(jnp.int32) - 1
        across = (cell >> 7).astype(f32)
        for half in range(HALVES):
            x_ref[half, here] = across - float(half * span)
        l_ref[here] = (cell & 127).astype(f32)
        cell = arrived.astype(jnp.int32) - 1
        bucket = jnp.where(cell < 0, BUCKETS, bucket_of(cell))
        slot = lax.broadcasted_iota(jnp.int32, (1, 128), 1).astype(f32) + float(h * 128)
        found = [
            jnp.max(jnp.where(bucket == b, 1.0, 0.0), axis=0, keepdims=True) for b in range(BUCKETS)
        ]
        found = jnp.concatenate(found, axis=0) > 0.0
        lows.append(jnp.where(found, slot, float(slots)))
        highs.append(jnp.where(found, slot + 1.0, 0.0))
    x_ref[:, slots:] = jnp.full((HALVES, x_ref.shape[1] - slots, 128), -512.0)
    l_ref[slots:] = jnp.zeros((l_ref.shape[0] - slots, 128), f32)
    value_ref[:, slots:] = jnp.zeros((8, value_ref.shape[1] - slots, 128), f32)
    low = jnp.min(jnp.minimum(lows[0], lows[1]), axis=1, keepdims=True)
    high = jnp.max(jnp.maximum(highs[0], highs[1]), axis=1, keepdims=True)
    low = (low.astype(jnp.int32) // STEP) * STEP
    rounds = (jnp.max(high.astype(jnp.int32) - low) + (STEP - 1)) // STEP
    firsts = [jnp.max(low[b : b + 1, :]) for b in range(BUCKETS)]
    total_ref[...] = jnp.zeros_like(total_ref)
    x_ids = lax.broadcasted_iota(jnp.int32, (span, 128), 0).astype(bf16)
    l_ids = [
        (lax.broadcasted_iota(jnp.int32, (lines, 128), 0) + g * lines).astype(bf16) for g in range(GROUPS)
    ]
    zero = jnp.zeros((), bf16)
    one = jnp.ones((), bf16)

    def step(t, carry):
        for b in range(BUCKETS):
            half, group = b // GROUPS, b % GROUPS
            first = pl.multiple_of(jnp.minimum(firsts[b] + t * STEP, slots), STEP)
            rows = pl.ds(first, STEP)
            x_rows, l_rows = x_ref[half, rows, :], l_ref[rows, :]
            value_rows = [value_ref[c, rows, :] for c in range(8)]
            sums = None
            for pair in range(STEP // PAIR):
                xs, values = [], []
                for k in range(pair * PAIR, (pair + 1) * PAIR):
                    xs.append(jnp.where(x_ids == spread(x_rows, k, span // 16), one, zero))
                    hot = l_ids[group] == spread(l_rows, k, lines // 16)
                    parts = [
                        jnp.where(hot, spread(value_rows[c], k, lines // 16), zero) for c in range(8)
                    ]
                    values.append(jnp.concatenate(parts, axis=0))
                xs = jnp.concatenate(xs, axis=1)
                part = dot_nt(jnp.concatenate(values, axis=1), xs)
                sums = part if sums is None else sums + part
            total_ref[b] += sums
        return carry

    lax.fori_loop(0, rounds, step, 0)
    for c in range(5):
        rate = rate_ref[c]
        if c == 0:
            out_ref[c] = rate
            continue
        for half in range(HALVES):
            parts = [
                total_ref[half * GROUPS + g, (c - 1) * lines : c * lines, :]
                + total_ref[half * GROUPS + g, (c + 3) * lines : (c + 4) * lines, :]
                for g in range(GROUPS)
            ]
            deposit = jnp.concatenate(parts, axis=0).T
            here = slice(half * span, (half + 1) * span)
            out_ref[c, here] = rate[here] - deposit


def along(block, distance):
    count = lax.axis_size("line")
    return lax.ppermute(block, "line", [(i, (i + distance) % count) for i in range(count)])


def run_fill(
    peers, grain_holding_processor, grain_mesh_slot, grain_speed_vector, fluid_speed_at_grain,
    thermal_states, grain_mass_over_lag,
):
    parts = grain_mesh_slot.shape[0]
    blocks = parts // 128
    return pl.pallas_call(
        fill_kernel,
        name="fill",
        compiler_params=pltpu.CompilerParams(vmem_limit_bytes=60 << 20),
        out_shape=jax.ShapeDtypeStruct((peers * 10, 128), f32),
        in_specs=[pl.BlockSpec(memory_space=pltpu.HBM)] * 7,
        cost_estimate=pl.CostEstimate(flops=12 * 10**9, bytes_accessed=10**6, transcendentals=0),
        scratch_shapes=[
            pltpu.VMEM((blocks, 128), jnp.int32),
            pltpu.VMEM((blocks, 128), jnp.int32),
            pltpu.VMEM((1, parts), jnp.int32),
            pltpu.VMEM((3, parts), f32),
            pltpu.VMEM((3, parts), f32),
            pltpu.VMEM((2, parts), f32),
            pltpu.VMEM((1, parts), f32),
            pltpu.SemaphoreType.DMA((7,)),
            pltpu.VMEM((8, parts), f32),
            pltpu.VMEM((8, parts), f32),
            pltpu.VMEM((blocks, 128), f32),
            pltpu.VMEM((blocks, peers, 128), bf16),
            pltpu.VMEM((blocks, BUCKETS, peers), f32),
            pltpu.VMEM((10 * peers, 256), f32),
        ],
    )(
        grain_holding_processor.reshape(blocks, 128),
        grain_mesh_slot.reshape(blocks, 128),
        grain_mesh_slot.reshape(1, parts),
        grain_speed_vector,
        fluid_speed_at_grain,
        thermal_states,
        grain_mass_over_lag.reshape(1, parts),
    )


def run_bin(arrived, rate):
    cells, lines = rate.shape[1:]
    return pl.pallas_call(
        bin_kernel,
        name="bin",
        compiler_params=pltpu.CompilerParams(vmem_limit_bytes=20 << 20),
        out_shape=jax.ShapeDtypeStruct((5, cells, lines), f32),
        scratch_shapes=[
            pltpu.VMEM((HALVES, 256 + 2 * STEP, 128), f32),
            pltpu.VMEM((256 + 2 * STEP, 128), f32),
            pltpu.VMEM((8, 256 + 2 * STEP, 128), f32),
            pltpu.VMEM((BUCKETS, 8 * lines // GROUPS, cells // HALVES), f32),
        ],
    )(arrived, rate)


def body(
    mass_per_volume,
    fluid_speed_field,
    fluid_thrust_field,
    shock_damping_field,
    grain_holding_processor,
    grain_mesh_slot,
    grain_speed_vector,
    fluid_speed_at_grain,
    thermal_states,
    grain_mass_over_lag,
):
    cells, lines = mass_per_volume.shape
    peers = lax.axis_size(("line", "slab"))
    blocks, probe, fix = operator_tables(cells)
    outgoing = run_fill(
        peers, grain_holding_processor, grain_mesh_slot, grain_speed_vector, fluid_speed_at_grain,
        thermal_states, grain_mass_over_lag,
    )
    arrived = lax.all_to_all(
        outgoing.reshape(peers, 5, 2, 128), ("line", "slab"), split_axis=0, concat_axis=0, tiled=True
    ).reshape(peers * 10, 128)

    gas = (mass_per_volume, fluid_speed_field, fluid_thrust_field, shock_damping_field)
    own, up, down, far_up, far_down = pl.pallas_call(
        edge_kernel,
        name="edge",
        compiler_params=pltpu.CompilerParams(vmem_limit_bytes=20 << 20),
        out_shape=(
            jax.ShapeDtypeStruct((cells, lines), f32),
            jax.ShapeDtypeStruct((96, lines), f32),
            jax.ShapeDtypeStruct((96, lines), f32),
            jax.ShapeDtypeStruct((8, lines), f32),
            jax.ShapeDtypeStruct((8, lines), f32),
        ),
        cost_estimate=pl.CostEstimate(flops=10**9, bytes_accessed=2 * 10**6, transcendentals=0),
    )(*gas, blocks, probe)
    left, right = along(up, 1), along(down, -1)
    far_left, far_right = along(far_up, 2), along(far_down, -2)
    rate = pl.pallas_call(
        flux_kernel,
        name="flux",
        compiler_params=pltpu.CompilerParams(vmem_limit_bytes=20 << 20),
        out_shape=jax.ShapeDtypeStruct((5, cells, lines), f32),
        cost_estimate=pl.CostEstimate(flops=2 * 10**9, bytes_accessed=4 * 10**6, transcendentals=0),
    )(*gas, own, up, down, left, right, far_left, far_right, blocks, fix)
    return run_bin(arrived, rate)


def solution(mesh):
    placed = (
        P("line", "slab"),
        P(None, "line", "slab"),
        P("line", "slab"),
        P("line", "slab"),
        P(("line", "slab"), None),
        P(("line", "slab")),
        P(None, ("line", "slab")),
        P(None, ("line", "slab")),
        P(None, ("line", "slab")),
        P(("line", "slab")),
    )
    step = jax.shard_map(
        body, mesh=mesh, in_specs=placed, out_specs=P(None, "line", "slab"), check_vma=False
    )
    return step
```

```python
import functools

import jax
import jax.numpy as jnp
import numpy as np
from jax import lax
from jax.experimental import pallas as pl
from jax.experimental.pallas import tpu as pltpu
from jax.sharding import PartitionSpec as P

band_one = 0.5
band_two = 0.05
rhs_one = 17.0 / 12.0
rhs_two = 101.0 / 150.0
rhs_three = 0.01
gamma_gas = 1.4
adiabatic_exponent = 0.6
highest = lax.Precision.HIGHEST
f32 = jnp.float32
bf16 = jnp.bfloat16

HALVES = 2
GROUPS = 4
BUCKETS = HALVES * GROUPS
STEP = 8
PAIR = 4
RING_SHIFT = 4
CHUNK = 16
FILL_PAIR = 4


def stacked_of(table):
    table = table.astype(np.float32)
    top = table.astype(jnp.bfloat16)
    rest = (table - top.astype(np.float32)).astype(jnp.bfloat16)
    return np.concatenate([top, rest, top], axis=1)


def operator_tables(cells):
    sums = np.roots([band_two, band_one, 1.0 - 2.0 * band_two]).real
    roots = np.array([(s + np.sqrt(s * s - 4.0)) / 2.0 for s in sums])
    roots = np.where(np.abs(roots) > 1.0, 1.0 / roots, roots)

    def right_side(z):
        return (
            rhs_one / 2.0 * (z - 1.0 / z)
            + rhs_two / 4.0 * (z**2 - z**-2)
            + rhs_three / 6.0 * (z**3 - z**-3)
        )

    weights = []
    for k in range(2):
        z, other = roots[k], roots[1 - k]
        slope = band_two * (z - 1.0 / z) * (z - other) * (z - 1.0 / other) / z
        weights.append(-right_side(z) / slope)
    direct = rhs_three / 6.0 / band_two
    place = np.arange(cells)
    reach = cells // 128
    blocks = []
    for apart in range(1 - reach, reach):
        offsets = 128 * apart + place[None, :128] - place[:128, None]
        sizes = np.abs(offsets)
        block = sum(w * z**sizes for w, z in zip(weights, roots))
        blocks.append(np.sign(offsets) * (block + direct * (sizes == 1)))
    blocks = np.concatenate(blocks)
    up, down = np.zeros((8, cells)), np.zeros((8, cells))
    low, high = np.zeros((cells, 8)), np.zeros((cells, 8))
    for k in range(2):
        up[k] = roots[k] ** (cells - 1 - place)
        down[k] = roots[k] ** place
        low[:, k] = -weights[k] * roots[k] ** (place + 1)
        high[:, k] = weights[k] * roots[k] ** (cells - place)
    up[2, cells - 1] = 1.0
    down[2, 0] = 1.0
    low[0, 2] = -direct
    high[cells - 1, 2] = direct
    probe = []
    for sums in (up, down):
        mixed = np.zeros((24, cells))
        for m in range(6):
            added = low[:, m] if m < 3 else high[:, m - 3]
            for k in range(3):
                mixed[(m // 2) * 8 + (m % 2) * 4 + k] = sums[k] * added
        probe += [sums, mixed]
    probe = np.concatenate(probe)
    fix = np.concatenate([low, high], axis=1)
    return stacked_of(blocks)[:, :256], stacked_of(probe), stacked_of(fix)


def halves_of(x):
    top = x.astype(bf16)
    return top, (x - top.astype(f32)).astype(bf16)


def dot_nn(a, b):
    return jnp.dot(a, b, preferred_element_type=f32)


def dot_nt(a, b):
    return lax.dot_general(a, b, (((1,), (1,)), ((), ())), preferred_element_type=f32)


def stack_of(x):
    top, rest = halves_of(x)
    return jnp.concatenate([top, top, rest], axis=0)


def operator_of(block_ref, cells):
    reach = cells // 128
    rows = []
    for i in range(reach):
        parts = []
        for part in (0, 1, 0):
            for j in range(reach):
                n = j - i + reach - 1
                parts.append(block_ref[n * 128 : (n + 1) * 128, part * 128 : (part + 1) * 128])
        rows.append(jnp.concatenate(parts, axis=1))
    return jnp.concatenate(rows, axis=0)


def fluxes_of(rho, vel_ref, thrust, damp, dilatation):
    u, v, w = vel_ref[0], vel_ref[1], vel_ref[2]
    pressure = thrust - damp * dilatation
    energy = thrust / (gamma_gas - 1.0) + 0.5 * rho * (u * u + v * v + w * w)
    momentum = rho * u
    return [
        momentum,
        momentum * u + pressure,
        momentum * v,
        momentum * w,
        (energy + pressure) * u,
    ]


def edge_kernel(
    rho_ref, vel_ref, thrust_ref, damp_ref, block_ref, probe_ref,
    own_ref, up_ref, down_ref, far_up_ref, far_down_ref,
):
    cells, lines = rho_ref.shape
    u, damp = vel_ref[0], damp_ref[...]
    own = dot_nn(operator_of(block_ref, cells), stack_of(u))
    own_ref[...] = own
    fields = [u] + fluxes_of(rho_ref[...], vel_ref, thrust_ref[...], damp, own) + [damp, damp * u]
    sums = dot_nn(probe_ref[...], stack_of(jnp.concatenate(fields, axis=1)))
    for first, out_ref, far_ref in ((0, up_ref, far_up_ref), (32, down_ref, far_down_ref)):
        for n in range(6):
            out_ref[n * 8 : (n + 1) * 8] = sums[first : first + 8, n * lines : (n + 1) * lines]
        for n in range(2):
            here = slice((6 + n) * lines, (7 + n) * lines)
            out_ref[48 + n * 24 : 72 + n * 24] = sums[first + 8 : first + 32, here]
        far_ref[...] = sums[first : first + 8, :lines]


def neighbour_sums(near_ref, low, high):
    mix = [low[m : m + 1] for m in range(3)] + [high[m : m + 1] for m in range(3)]
    wide = [jnp.broadcast_to(row, (4, row.shape[1])) for row in mix]
    found = []
    for c in range(5):
        base = near_ref[(1 + c) * 8 : (2 + c) * 8]
        if c in (1, 4):
            first = 48 if c == 1 else 72
            added = sum(
                near_ref[first + q * 8 : first + (q + 1) * 8]
                * jnp.concatenate([wide[2 * q], wide[2 * q + 1]], axis=0)
                for q in range(3)
            )
            base = base - added - pltpu.roll(added, 4, 0)
        found.append(base)
    return jnp.concatenate(found, axis=1)


def flux_kernel(
    rho_ref, vel_ref, thrust_ref, damp_ref, own_ref, up_ref, down_ref,
    left_ref, right_ref, far_left_ref, far_right_ref, block_ref, fix_ref, rate_ref,
):
    cells, lines = rho_ref.shape
    full = operator_of(block_ref, cells)
    near = jnp.concatenate([left_ref[:8], right_ref[:8]], axis=0)
    dilatation = own_ref[...] + dot_nn(fix_ref[...], stack_of(near))
    fluxes = fluxes_of(rho_ref[...], vel_ref, thrust_ref[...], damp_ref[...], dilatation)
    sums = jnp.concatenate(
        [
            neighbour_sums(left_ref, far_left_ref[...], down_ref[:8]),
            neighbour_sums(right_ref, up_ref[:8], far_right_ref[...]),
        ],
        axis=0,
    )
    added = dot_nn(fix_ref[...], stack_of(sums))
    for group in ((0, 1), (2, 3), (4,)):
        field = jnp.concatenate([fluxes[c] for c in group], axis=1)
        done = dot_nn(full, stack_of(field))
        for n, c in enumerate(group):
            rate_ref[c] = -(
                done[:, n * lines : (n + 1) * lines] + added[:, c * lines : (c + 1) * lines]
            )


def spread(block, k, copies):
    wide = jnp.broadcast_to(block[k : k + 1, :], (16, 128)).astype(bf16)
    return jnp.concatenate([wide] * copies, axis=0)


def wrapped(slot):
    slot = jnp.where(slot >= 256.0, slot - 256.0, slot)
    return jnp.where(slot < 0.0, slot + 256.0, slot)


def bucket_of(cell):
    return (cell >> 15) * GROUPS + ((cell & 127) >> 5)


def fill_kernel(
    *refs,
):
    sources, out_ref, targets, sems = refs[:7], refs[7], refs[8:15], refs[15]
    top_ref, rest_ref, key_ref, hot_ref, count_ref, total_ref = refs[16:]
    peers_ref, cells_ref, cell_ref, speed_ref, fluid_ref, thermal_ref, mass_ref = targets
    copies = [
        pltpu.make_async_copy(source, target, sems.at[n])
        for n, (source, target) in enumerate(zip(sources, targets))
    ]
    for copy in copies:
        copy.start()
    for copy in copies:
        copy.wait()
    peers = out_ref.shape[0] // 10
    blocks = peers_ref.shape[0]
    mass = mass_ref[...]
    work = adiabatic_exponent * mass * (thermal_ref[1:2, :] - thermal_ref[0:1, :])
    rows = []
    for c in range(3):
        speed = speed_ref[c : c + 1, :]
        force = mass * (fluid_ref[c : c + 1, :] - speed)
        work = work + force * speed
        rows.append(force)
    rows.append(work)
    rows.append((cell_ref[...] + 1).astype(f32))
    for c in range(5):
        top = rows[c].astype(bf16).astype(f32)
        top_ref[c : c + 1, :] = top
        rest_ref[c : c + 1, :] = rows[c] - top

    keys = (peers_ref[...] * BUCKETS + bucket_of(cells_ref[...])).astype(f32)
    key_ref[...] = keys
    turned = jnp.concatenate([keys, keys], axis=0).T
    peer_ids = lax.broadcasted_iota(jnp.int32, (peers, 128), 0).astype(bf16)
    bucket_ids = lax.broadcasted_iota(jnp.int32, (BUCKETS, 128), 0)
    earlier = lax.broadcasted_iota(jnp.int32, (128, 128), 0) < lax.broadcasted_iota(jnp.int32, (128, 128), 1)
    slot_ids = lax.broadcasted_iota(jnp.int32, (256, 128), 0).astype(bf16)
    zero = jnp.zeros((), bf16)
    one = jnp.ones((), bf16)

    def buckets_at(block, k):
        return block[k : k + 1, :] == bucket_ids

    def count_step(t, carry):
        for n in range(2):
            rows = pl.ds(pl.multiple_of((2 * t + n) * CHUNK, CHUNK), CHUNK)
            peer_rows = peers_ref[rows, :].astype(f32)
            bucket_rows = bucket_of(cells_ref[rows, :])
            for k in range(CHUNK):
                i = (2 * t + n) * CHUNK + k
                hot = jnp.where(peer_ids == spread(peer_rows, k, peers // 16), one, zero)
                hot_ref[i] = hot
                mine = jnp.where(buckets_at(bucket_rows, k), 1.0, 0.0).astype(bf16)
                count_ref[i] = dot_nt(mine, hot)
        return carry

    lax.fori_loop(0, blocks // (2 * CHUNK), count_step, 0)

    def base_step(t, before):
        for k in range(CHUNK):
            now = count_ref[t * CHUNK + k]
            count_ref[t * CHUNK + k] = before
            before = before + now
        return before

    counts = lax.fori_loop(0, blocks // CHUNK, base_step, jnp.zeros((BUCKETS, 128), f32))
    room = [None] * BUCKETS
    left = jnp.full((1, 128), 256.0)
    for b in reversed(range(BUCKETS)):
        left = left - counts[b : b + 1, :]
        room[b] = left
    starts = []
    end = jnp.zeros((1, 128), f32)
    for b in range(BUCKETS):
        starts.append(jnp.minimum(jnp.maximum(end, float(b * 256 // BUCKETS)), room[b]))
        end = starts[-1] + counts[b : b + 1, :]
    drifts = [starts[b] - float(b * 256 // BUCKETS) for b in range(BUCKETS)]
    turn = float(RING_SHIFT) - jnp.floor(
        (functools.reduce(jnp.maximum, drifts) + functools.reduce(jnp.minimum, drifts)) * 0.5
    )
    start = jnp.concatenate([wrapped(x + turn) for x in starts], axis=0)

    rounds = blocks // CHUNK

    def rank_rows(t, rolled):
        rows = pl.ds(pl.multiple_of(t * CHUNK, CHUNK), CHUNK)
        key_rows = key_ref[rows, :]
        bucket_rows = bucket_of(cells_ref[rows, :])
        ranks = []
        for k in range(CHUNK):
            i = t * CHUNK + k
            same = (rolled[:, k : k + 1] == key_rows[k : k + 1, :]) & earlier
            inside = jnp.sum(jnp.where(same, 1.0, 0.0), axis=0, keepdims=True)
            base = dot_nn(wrapped(count_ref[i] + start).astype(bf16), hot_ref[i])
            base = jnp.sum(jnp.where(buckets_at(bucket_rows, k), base, 0.0), axis=0, keepdims=True)
            ranks.append(wrapped(base + inside))
        return jnp.concatenate(ranks, axis=0), pltpu.roll(rolled, 128 - CHUNK, 1)

    total_ref[...] = jnp.zeros_like(total_ref)

    def place_step(t, carry):
        rank_rows_now, rolled = carry
        rows = pl.ds(pl.multiple_of(t * CHUNK, CHUNK), CHUNK)
        peer_rows = peers_ref[rows, :].astype(f32)
        sums = None
        for pair in range(CHUNK // FILL_PAIR):
            ranks, values = [], []
            for k in range(pair * FILL_PAIR, (pair + 1) * FILL_PAIR):
                here = pl.ds(pl.multiple_of((t * CHUNK + k) * 128, 128), 128)
                ranks.append(jnp.where(slot_ids == spread(rank_rows_now, k, 16), one, zero))
                hot = peer_ids == spread(peer_rows, k, peers // 16)
                top_rows, rest_rows = top_ref[:, here], rest_ref[:, here]
                parts = [jnp.where(hot, spread(top_rows, c, peers // 16), zero) for c in range(5)]
                parts += [jnp.where(hot, spread(rest_rows, c, peers // 16), zero) for c in range(5)]
                values.append(jnp.concatenate(parts, axis=0))
            ranks = jnp.concatenate(ranks, axis=1)
            part = dot_nt(jnp.concatenate(values, axis=1), ranks)
            sums = part if sums is None else sums + part
        following = rank_rows(jnp.minimum(t + 1, rounds - 1), rolled)
        total_ref[...] += sums
        return following

    lax.fori_loop(0, rounds, place_step, rank_rows(0, turned))
    for c in range(5):
        for h in range(2):
            here = slice(h * 128, (h + 1) * 128)
            out_ref[pl.ds(2 * c + h, peers, stride=10), :] = (
                total_ref[c * peers : (c + 1) * peers, here]
                + total_ref[(c + 5) * peers : (c + 6) * peers, here]
            )


def bin_kernel(
    box_ref, rate_ref, out_ref, x_ref, l_ref, value_ref, total_ref, done_ref, sems,
):
    mass_copy = pltpu.make_async_copy(rate_ref.at[0], out_ref.at[0], sems.at[0])
    mass_copy.start()
    span = out_ref.shape[1] // HALVES
    lines = out_ref.shape[2] // GROUPS
    slots = 256
    lows, highs = [], []
    for h in range(2):
        here = slice(h * 128, (h + 1) * 128)
        for c in range(4):
            value = box_ref[pl.ds(2 * c + h, 128, stride=10), :].T
            top = value.astype(bf16).astype(f32)
            value_ref[c, here] = top
            value_ref[4 + c, here] = value - top
        arrived = box_ref[pl.ds(8 + h, 128, stride=10), :]
        cell = arrived.T.astype(jnp.int32) - 1
        across = (cell >> 7).astype(f32)
        for half in range(HALVES):
            x_ref[half, here] = across - float(half * span)
        l_ref[here] = (cell & 127).astype(f32)
        cell = arrived.astype(jnp.int32) - 1
        bucket = jnp.where(cell < 0, BUCKETS, bucket_of(cell))
        slot = lax.broadcasted_iota(jnp.int32, (BUCKETS, 128), 1) + h * 128
        share = lax.broadcasted_iota(jnp.int32, (BUCKETS, 128), 0) * (slots // BUCKETS)
        slot = (((slot - share + slots // 2) & (slots - 1)) - slots // 2).astype(f32)
        found = [
            jnp.max(jnp.where(bucket == b, 1.0, 0.0), axis=0, keepdims=True) for b in range(BUCKETS)
        ]
        found = jnp.concatenate(found, axis=0) > 0.0
        lows.append(jnp.where(found, slot, float(slots)))
        highs.append(jnp.where(found, slot + 1.0, -float(slots)))
    low = jnp.floor(jnp.min(jnp.minimum(lows[0], lows[1]), axis=1, keepdims=True) * (1.0 / STEP))
    high = jnp.max(jnp.maximum(highs[0], highs[1]), axis=1, keepdims=True)
    rounds = (jnp.max(high - low * STEP).astype(jnp.int32) + (STEP - 1)) // STEP
    low = jnp.minimum(low, float(slots // STEP)) + float(slots // 2 // STEP)
    index = lax.broadcasted_iota(jnp.int32, (BUCKETS, 1), 0)
    weight = jnp.where(
        index % 4 == 0, 1.0, jnp.where(index % 4 == 1, 64.0, jnp.where(index % 4 == 2, 4096.0, 262144.0))
    )
    firsts = []
    for part in (0, 1):
        packed = jnp.sum(jnp.where(index // 4 == part, low * weight, 0.0)).astype(jnp.int32)
        firsts += [(packed >> (6 * n)) & 63 for n in range(4)]
    total_ref[...] = jnp.zeros_like(total_ref)
    x_ids = lax.broadcasted_iota(jnp.int32, (span, 128), 0).astype(bf16)
    l_ids = [
        (lax.broadcasted_iota(jnp.int32, (lines, 128), 0) + g * lines).astype(bf16) for g in range(GROUPS)
    ]
    zero = jnp.zeros((), bf16)
    one = jnp.ones((), bf16)

    def step(t, carry):
        for b in range(BUCKETS):
            half, group = b // GROUPS, b % GROUPS
            share = b * (slots // BUCKETS // STEP) - slots // 2 // STEP
            first = ((firsts[b] + share + t) & (slots // STEP - 1)) * STEP
            rows = pl.ds(pl.multiple_of(first, STEP), STEP)
            x_rows, l_rows = x_ref[half, rows, :], l_ref[rows, :]
            value_rows = [value_ref[c, rows, :] for c in range(8)]
            sums = None
            for pair in range(STEP // PAIR):
                xs, values = [], []
                for k in range(pair * PAIR, (pair + 1) * PAIR):
                    xs.append(jnp.where(x_ids == spread(x_rows, k, span // 16), one, zero))
                    hot = l_ids[group] == spread(l_rows, k, lines // 16)
                    parts = [
                        jnp.where(hot, spread(value_rows[c], k, lines // 16), zero) for c in range(8)
                    ]
                    values.append(jnp.concatenate(parts, axis=0))
                xs = jnp.concatenate(xs, axis=1)
                part = dot_nt(jnp.concatenate(values, axis=1), xs)
                sums = part if sums is None else sums + part
            total_ref[b] += sums
        return carry

    lax.fori_loop(0, rounds, step, 0)
    copies = []
    for c in range(1, 5):
        for half in range(HALVES):
            parts = [
                total_ref[half * GROUPS + g, (c - 1) * lines : c * lines, :]
                + total_ref[half * GROUPS + g, (c + 3) * lines : (c + 4) * lines, :]
                for g in range(GROUPS)
            ]
            deposit = jnp.concatenate(parts, axis=0).T
            here = slice(half * span, (half + 1) * span)
            done_ref[c - 1, here] = rate_ref[c, here] - deposit
        copies.append(pltpu.make_async_copy(done_ref.at[c - 1], out_ref.at[c], sems.at[c]))
        copies[-1].start()
    for copy in copies:
        copy.wait()
    mass_copy.wait()


def along(block, distance):
    count = lax.axis_size("line")
    return lax.ppermute(block, "line", [(i, (i + distance) % count) for i in range(count)])


def run_fill(
    peers, grain_holding_processor, grain_mesh_slot, grain_speed_vector, fluid_speed_at_grain,
    thermal_states, grain_mass_over_lag,
):
    parts = grain_mesh_slot.shape[0]
    blocks = parts // 128
    return pl.pallas_call(
        fill_kernel,
        name="fill",
        compiler_params=pltpu.CompilerParams(vmem_limit_bytes=60 << 20),
        out_shape=jax.ShapeDtypeStruct((peers * 10, 128), f32),
        in_specs=[pl.BlockSpec(memory_space=pltpu.HBM)] * 7,
        cost_estimate=pl.CostEstimate(flops=12 * 10**9, bytes_accessed=10**6, transcendentals=0),
        scratch_shapes=[
            pltpu.VMEM((blocks, 128), jnp.int32),
            pltpu.VMEM((blocks, 128), jnp.int32),
            pltpu.VMEM((1, parts), jnp.int32),
            pltpu.VMEM((3, parts), f32),
            pltpu.VMEM((3, parts), f32),
            pltpu.VMEM((2, parts), f32),
            pltpu.VMEM((1, parts), f32),
            pltpu.SemaphoreType.DMA((7,)),
            pltpu.VMEM((8, parts), f32),
            pltpu.VMEM((8, parts), f32),
            pltpu.VMEM((blocks, 128), f32),
            pltpu.VMEM((blocks, peers, 128), bf16),
            pltpu.VMEM((blocks, BUCKETS, peers), f32),
            pltpu.VMEM((10 * peers, 256), f32),
        ],
    )(
        grain_holding_processor.reshape(blocks, 128),
        grain_mesh_slot.reshape(blocks, 128),
        grain_mesh_slot.reshape(1, parts),
        grain_speed_vector,
        fluid_speed_at_grain,
        thermal_states,
        grain_mass_over_lag.reshape(1, parts),
    )


def run_bin(arrived, rate):
    cells, lines = rate.shape[1:]
    return pl.pallas_call(
        bin_kernel,
        name="bin",
        compiler_params=pltpu.CompilerParams(vmem_limit_bytes=20 << 20),
        out_shape=jax.ShapeDtypeStruct((5, cells, lines), f32),
        in_specs=[pl.BlockSpec(memory_space=pltpu.VMEM)] * 2,
        out_specs=pl.BlockSpec(memory_space=pltpu.HBM),
        scratch_shapes=[
            pltpu.VMEM((HALVES, 256, 128), f32),
            pltpu.VMEM((256, 128), f32),
            pltpu.VMEM((8, 256, 128), f32),
            pltpu.VMEM((BUCKETS, 8 * lines // GROUPS, cells // HALVES), f32),
            pltpu.VMEM((4, cells, lines), f32),
            pltpu.SemaphoreType.DMA((5,)),
        ],
    )(arrived, rate)


def body(
    mass_per_volume,
    fluid_speed_field,
    fluid_thrust_field,
    shock_damping_field,
    grain_holding_processor,
    grain_mesh_slot,
    grain_speed_vector,
    fluid_speed_at_grain,
    thermal_states,
    grain_mass_over_lag,
):
    cells, lines = mass_per_volume.shape
    peers = lax.axis_size(("line", "slab"))
    blocks, probe, fix = operator_tables(cells)
    outgoing = run_fill(
        peers, grain_holding_processor, grain_mesh_slot, grain_speed_vector, fluid_speed_at_grain,
        thermal_states, grain_mass_over_lag,
    )
    arrived = lax.all_to_all(
        outgoing.reshape(peers, 5, 2, 128), ("line", "slab"), split_axis=0, concat_axis=0, tiled=True
    ).reshape(peers * 10, 128)

    gas = (mass_per_volume, fluid_speed_field, fluid_thrust_field, shock_damping_field)
    own, up, down, far_up, far_down = pl.pallas_call(
        edge_kernel,
        name="edge",
        compiler_params=pltpu.CompilerParams(vmem_limit_bytes=20 << 20),
        out_shape=(
            jax.ShapeDtypeStruct((cells, lines), f32),
            jax.ShapeDtypeStruct((96, lines), f32),
            jax.ShapeDtypeStruct((96, lines), f32),
            jax.ShapeDtypeStruct((8, lines), f32),
            jax.ShapeDtypeStruct((8, lines), f32),
        ),
        cost_estimate=pl.CostEstimate(flops=10**9, bytes_accessed=2 * 10**6, transcendentals=0),
    )(*gas, blocks, probe)
    left, right = along(up, 1), along(down, -1)
    far_left, far_right = along(far_up, 2), along(far_down, -2)
    rate = pl.pallas_call(
        flux_kernel,
        name="flux",
        compiler_params=pltpu.CompilerParams(vmem_limit_bytes=20 << 20),
        out_shape=jax.ShapeDtypeStruct((5, cells, lines), f32),
        cost_estimate=pl.CostEstimate(flops=2 * 10**9, bytes_accessed=4 * 10**6, transcendentals=0),
    )(*gas, own, up, down, left, right, far_left, far_right, blocks, fix)
    return run_bin(arrived, rate)


def solution(mesh):
    placed = (
        P("line", "slab"),
        P(None, "line", "slab"),
        P("line", "slab"),
        P("line", "slab"),
        P(("line", "slab"), None),
        P(("line", "slab")),
        P(None, ("line", "slab")),
        P(None, ("line", "slab")),
        P(None, ("line", "slab")),
        P(("line", "slab")),
    )
    step = jax.shard_map(
        body, mesh=mesh, in_specs=placed, out_specs=P(None, "line", "slab"), check_vma=False
    )
    return step
```

```python
import functools

import jax
import jax.numpy as jnp
import numpy as np
from jax import lax
from jax.experimental import pallas as pl
from jax.experimental.pallas import tpu as pltpu
from jax.sharding import PartitionSpec as P

band_one = 0.5
band_two = 0.05
rhs_one = 17.0 / 12.0
rhs_two = 101.0 / 150.0
rhs_three = 0.01
gamma_gas = 1.4
adiabatic_exponent = 0.6
highest = lax.Precision.HIGHEST
f32 = jnp.float32
bf16 = jnp.bfloat16

HALVES = 2
GROUPS = 4
BUCKETS = HALVES * GROUPS
STEP = 8
PAIR = 4
RING_SHIFT = 4
CHUNK = 32
FILL_PAIR = 4


def stacked_of(table):
    table = table.astype(np.float32)
    top = table.astype(jnp.bfloat16)
    rest = (table - top.astype(np.float32)).astype(jnp.bfloat16)
    return np.concatenate([top, rest, top], axis=1)


def operator_tables(cells):
    sums = np.roots([band_two, band_one, 1.0 - 2.0 * band_two]).real
    roots = np.array([(s + np.sqrt(s * s - 4.0)) / 2.0 for s in sums])
    roots = np.where(np.abs(roots) > 1.0, 1.0 / roots, roots)

    def right_side(z):
        return (
            rhs_one / 2.0 * (z - 1.0 / z)
            + rhs_two / 4.0 * (z**2 - z**-2)
            + rhs_three / 6.0 * (z**3 - z**-3)
        )

    weights = []
    for k in range(2):
        z, other = roots[k], roots[1 - k]
        slope = band_two * (z - 1.0 / z) * (z - other) * (z - 1.0 / other) / z
        weights.append(-right_side(z) / slope)
    direct = rhs_three / 6.0 / band_two
    place = np.arange(cells)
    reach = cells // 128
    blocks = []
    for apart in range(1 - reach, reach):
        offsets = 128 * apart + place[None, :128] - place[:128, None]
        sizes = np.abs(offsets)
        block = sum(w * z**sizes for w, z in zip(weights, roots))
        blocks.append(np.sign(offsets) * (block + direct * (sizes == 1)))
    blocks = np.concatenate(blocks)
    up, down = np.zeros((8, cells)), np.zeros((8, cells))
    low, high = np.zeros((cells, 8)), np.zeros((cells, 8))
    for k in range(2):
        up[k] = roots[k] ** (cells - 1 - place)
        down[k] = roots[k] ** place
        low[:, k] = -weights[k] * roots[k] ** (place + 1)
        high[:, k] = weights[k] * roots[k] ** (cells - place)
    up[2, cells - 1] = 1.0
    down[2, 0] = 1.0
    low[0, 2] = -direct
    high[cells - 1, 2] = direct
    probe = []
    for sums in (up, down):
        mixed = np.zeros((24, cells))
        for m in range(6):
            added = low[:, m] if m < 3 else high[:, m - 3]
            for k in range(3):
                mixed[(m // 2) * 8 + (m % 2) * 4 + k] = sums[k] * added
        probe += [sums, mixed]
    probe = np.concatenate(probe)
    fix = np.concatenate([low, high], axis=1)
    return stacked_of(blocks)[:, :256], stacked_of(probe), stacked_of(fix)


def halves_of(x):
    top = x.astype(bf16)
    return top, (x - top.astype(f32)).astype(bf16)


def dot_nn(a, b):
    return jnp.dot(a, b, preferred_element_type=f32)


def dot_nt(a, b):
    return lax.dot_general(a, b, (((1,), (1,)), ((), ())), preferred_element_type=f32)


def stack_of(x):
    top, rest = halves_of(x)
    return jnp.concatenate([top, top, rest], axis=0)


def operator_of(block_ref, cells):
    reach = cells // 128
    rows = []
    for i in range(reach):
        parts = []
        for part in (0, 1, 0):
            for j in range(reach):
                n = j - i + reach - 1
                parts.append(block_ref[n * 128 : (n + 1) * 128, part * 128 : (part + 1) * 128])
        rows.append(jnp.concatenate(parts, axis=1))
    return jnp.concatenate(rows, axis=0)


def fluxes_of(rho, vel_ref, thrust, damp, dilatation):
    u, v, w = vel_ref[0], vel_ref[1], vel_ref[2]
    pressure = thrust - damp * dilatation
    energy = thrust / (gamma_gas - 1.0) + 0.5 * rho * (u * u + v * v + w * w)
    momentum = rho * u
    return [
        momentum,
        momentum * u + pressure,
        momentum * v,
        momentum * w,
        (energy + pressure) * u,
    ]


def edge_kernel(
    rho_ref, vel_ref, thrust_ref, damp_ref, block_ref, probe_ref,
    own_ref, up_ref, down_ref, far_up_ref, far_down_ref,
):
    cells, lines = rho_ref.shape
    u, damp = vel_ref[0], damp_ref[...]
    own = dot_nn(operator_of(block_ref, cells), stack_of(u))
    own_ref[...] = own
    fields = [u] + fluxes_of(rho_ref[...], vel_ref, thrust_ref[...], damp, own) + [damp, damp * u]
    sums = dot_nn(probe_ref[...], stack_of(jnp.concatenate(fields, axis=1)))
    for first, out_ref, far_ref in ((0, up_ref, far_up_ref), (32, down_ref, far_down_ref)):
        for n in range(6):
            out_ref[n * 8 : (n + 1) * 8] = sums[first : first + 8, n * lines : (n + 1) * lines]
        for n in range(2):
            here = slice((6 + n) * lines, (7 + n) * lines)
            out_ref[48 + n * 24 : 72 + n * 24] = sums[first + 8 : first + 32, here]
        far_ref[...] = sums[first : first + 8, :lines]


def neighbour_sums(near_ref, low, high):
    mix = [low[m : m + 1] for m in range(3)] + [high[m : m + 1] for m in range(3)]
    wide = [jnp.broadcast_to(row, (4, row.shape[1])) for row in mix]
    found = []
    for c in range(5):
        base = near_ref[(1 + c) * 8 : (2 + c) * 8]
        if c in (1, 4):
            first = 48 if c == 1 else 72
            added = sum(
                near_ref[first + q * 8 : first + (q + 1) * 8]
                * jnp.concatenate([wide[2 * q], wide[2 * q + 1]], axis=0)
                for q in range(3)
            )
            base = base - added - pltpu.roll(added, 4, 0)
        found.append(base)
    return jnp.concatenate(found, axis=1)


def flux_kernel(
    rho_ref, vel_ref, thrust_ref, damp_ref, own_ref, up_ref, down_ref,
    left_ref, right_ref, far_left_ref, far_right_ref, block_ref, fix_ref, rate_ref,
):
    cells, lines = rho_ref.shape
    full = operator_of(block_ref, cells)
    near = jnp.concatenate([left_ref[:8], right_ref[:8]], axis=0)
    dilatation = own_ref[...] + dot_nn(fix_ref[...], stack_of(near))
    fluxes = fluxes_of(rho_ref[...], vel_ref, thrust_ref[...], damp_ref[...], dilatation)
    sums = jnp.concatenate(
        [
            neighbour_sums(left_ref, far_left_ref[...], down_ref[:8]),
            neighbour_sums(right_ref, up_ref[:8], far_right_ref[...]),
        ],
        axis=0,
    )
    added = dot_nn(fix_ref[...], stack_of(sums))
    for group in ((0, 1), (2, 3), (4,)):
        field = jnp.concatenate([fluxes[c] for c in group], axis=1)
        done = dot_nn(full, stack_of(field))
        for n, c in enumerate(group):
            rate_ref[c] = -(
                done[:, n * lines : (n + 1) * lines] + added[:, c * lines : (c + 1) * lines]
            )


def spread(block, k, copies):
    wide = jnp.broadcast_to(block[k : k + 1, :], (16, 128)).astype(bf16)
    return jnp.concatenate([wide] * copies, axis=0)


def wrapped(slot):
    slot = jnp.where(slot >= 256.0, slot - 256.0, slot)
    return jnp.where(slot < 0.0, slot + 256.0, slot)


def bucket_of(cell):
    return (cell >> 15) * GROUPS + ((cell & 127) >> 5)


def fill_kernel(
    *refs,
):
    sources, out_ref, targets, sems = refs[:7], refs[7], refs[8:15], refs[15]
    top_ref, rest_ref, key_ref, hot_ref, count_ref, total_ref = refs[16:]
    peers_ref, cells_ref, cell_ref, speed_ref, fluid_ref, thermal_ref, mass_ref = targets
    copies = [
        pltpu.make_async_copy(source, target, sems.at[n])
        for n, (source, target) in enumerate(zip(sources, targets))
    ]
    for copy in copies:
        copy.start()
    for copy in copies[:2]:
        copy.wait()
    peers = out_ref.shape[0] // 10
    blocks = peers_ref.shape[0]
    keys = (peers_ref[...] * BUCKETS + bucket_of(cells_ref[...])).astype(f32)
    key_ref[...] = keys
    turned = jnp.concatenate([keys, keys], axis=0).T
    peer_ids = lax.broadcasted_iota(jnp.int32, (peers, 128), 0).astype(bf16)
    bucket_ids = lax.broadcasted_iota(jnp.int32, (BUCKETS, 128), 0)
    earlier = lax.broadcasted_iota(jnp.int32, (128, 128), 0) < lax.broadcasted_iota(jnp.int32, (128, 128), 1)
    slot_ids = lax.broadcasted_iota(jnp.int32, (256, 128), 0).astype(bf16)
    zero = jnp.zeros((), bf16)
    one = jnp.ones((), bf16)

    def buckets_at(block, k):
        return block[k : k + 1, :] == bucket_ids

    def count_step(t, carry):
        for n in range(2):
            rows = pl.ds(pl.multiple_of((2 * t + n) * CHUNK, CHUNK), CHUNK)
            peer_rows = peers_ref[rows, :].astype(f32)
            bucket_rows = bucket_of(cells_ref[rows, :])
            for k in range(0, CHUNK, 2):
                i = (2 * t + n) * CHUNK + k
                mine, hots = [], []
                for m in range(2):
                    hots.append(jnp.where(peer_ids == spread(peer_rows, k + m, peers // 16), one, zero))
                    hot_ref[i + m] = hots[m]
                    here = jnp.where(buckets_at(bucket_rows, k + m), 1.0, 0.0)
                    none = jnp.zeros_like(here)
                    mine.append(jnp.concatenate([none, here] if m else [here, none], axis=1))
                found = dot_nt(
                    jnp.concatenate(mine, axis=0).astype(bf16), jnp.concatenate(hots, axis=1)
                )
                count_ref[i], count_ref[i + 1] = found[:BUCKETS], found[BUCKETS:]
        return carry

    lax.fori_loop(0, blocks // (2 * CHUNK), count_step, 0)

    def base_step(t, before):
        for k in range(CHUNK):
            now = count_ref[t * CHUNK + k]
            count_ref[t * CHUNK + k] = before
            before = before + now
        return before

    counts = lax.fori_loop(0, blocks // CHUNK, base_step, jnp.zeros((BUCKETS, 128), f32))
    room = [None] * BUCKETS
    left = jnp.full((1, 128), 256.0)
    for b in reversed(range(BUCKETS)):
        left = left - counts[b : b + 1, :]
        room[b] = left
    starts = []
    end = jnp.zeros((1, 128), f32)
    for b in range(BUCKETS):
        starts.append(jnp.minimum(jnp.maximum(end, float(b * 256 // BUCKETS)), room[b]))
        end = starts[-1] + counts[b : b + 1, :]
    drifts = [starts[b] - float(b * 256 // BUCKETS) for b in range(BUCKETS)]
    turn = float(RING_SHIFT) - jnp.floor(
        (functools.reduce(jnp.maximum, drifts) + functools.reduce(jnp.minimum, drifts)) * 0.5
    )
    start = jnp.concatenate([wrapped(x + turn) for x in starts], axis=0)

    rounds = blocks // CHUNK

    def rank_rows(t, rolled):
        rows = pl.ds(pl.multiple_of(t * CHUNK, CHUNK), CHUNK)
        key_rows = key_ref[rows, :]
        bucket_rows = bucket_of(cells_ref[rows, :])
        ranks = []
        for k in range(CHUNK):
            i = t * CHUNK + k
            same = (rolled[:, k : k + 1] == key_rows[k : k + 1, :]) & earlier
            inside = jnp.sum(jnp.where(same, 1.0, 0.0), axis=0, keepdims=True)
            base = dot_nn(wrapped(count_ref[i] + start).astype(bf16), hot_ref[i])
            base = jnp.sum(jnp.where(buckets_at(bucket_rows, k), base, 0.0), axis=0, keepdims=True)
            ranks.append(wrapped(base + inside))
        return jnp.concatenate(ranks, axis=0), pltpu.roll(rolled, 128 - CHUNK, 1)

    for copy in copies[2:]:
        copy.wait()
    mass = mass_ref[...]
    work = adiabatic_exponent * mass * (thermal_ref[1:2, :] - thermal_ref[0:1, :])
    rows = []
    for c in range(3):
        speed = speed_ref[c : c + 1, :]
        force = mass * (fluid_ref[c : c + 1, :] - speed)
        work = work + force * speed
        rows.append(force)
    rows.append(work)
    rows.append((cell_ref[...] + 1).astype(f32))
    for c in range(5):
        top = rows[c].astype(bf16).astype(f32)
        top_ref[c : c + 1, :] = top
        rest_ref[c : c + 1, :] = rows[c] - top
    total_ref[...] = jnp.zeros_like(total_ref)

    def place_step(t, carry):
        rank_rows_now, rolled = carry
        rows = pl.ds(pl.multiple_of(t * CHUNK, CHUNK), CHUNK)
        peer_rows = peers_ref[rows, :].astype(f32)
        sums = None
        for pair in range(CHUNK // FILL_PAIR):
            ranks, values = [], []
            for k in range(pair * FILL_PAIR, (pair + 1) * FILL_PAIR):
                here = pl.ds(pl.multiple_of((t * CHUNK + k) * 128, 128), 128)
                ranks.append(jnp.where(slot_ids == spread(rank_rows_now, k, 16), one, zero))
                hot = peer_ids == spread(peer_rows, k, peers // 16)
                top_rows, rest_rows = top_ref[:, here], rest_ref[:, here]
                parts = [jnp.where(hot, spread(top_rows, c, peers // 16), zero) for c in range(5)]
                parts += [jnp.where(hot, spread(rest_rows, c, peers // 16), zero) for c in range(5)]
                values.append(jnp.concatenate(parts, axis=0))
            ranks = jnp.concatenate(ranks, axis=1)
            part = dot_nt(jnp.concatenate(values, axis=1), ranks)
            sums = part if sums is None else sums + part
        following = rank_rows(jnp.minimum(t + 1, rounds - 1), rolled)
        total_ref[...] += sums
        return following

    lax.fori_loop(0, rounds, place_step, rank_rows(0, turned))
    for c in range(5):
        for h in range(2):
            here = slice(h * 128, (h + 1) * 128)
            out_ref[pl.ds(2 * c + h, peers, stride=10), :] = (
                total_ref[c * peers : (c + 1) * peers, here]
                + total_ref[(c + 5) * peers : (c + 6) * peers, here]
            )


def bin_kernel(
    box_ref, rate_ref, out_ref, x_ref, l_ref, value_ref, total_ref, done_ref, sems,
):
    mass_copy = pltpu.make_async_copy(rate_ref.at[0], out_ref.at[0], sems.at[0])
    mass_copy.start()
    span = out_ref.shape[1] // HALVES
    lines = out_ref.shape[2] // GROUPS
    slots = 256
    lows, highs = [], []
    for h in range(2):
        here = slice(h * 128, (h + 1) * 128)
        for c in range(4):
            value = box_ref[pl.ds(2 * c + h, 128, stride=10), :].T
            top = value.astype(bf16).astype(f32)
            value_ref[c, here] = top
            value_ref[4 + c, here] = value - top
        arrived = box_ref[pl.ds(8 + h, 128, stride=10), :]
        cell = arrived.T.astype(jnp.int32) - 1
        across = (cell >> 7).astype(f32)
        for half in range(HALVES):
            x_ref[half, here] = across - float(half * span)
        l_ref[here] = (cell & 127).astype(f32)
        cell = arrived.astype(jnp.int32) - 1
        bucket = jnp.where(cell < 0, BUCKETS, bucket_of(cell))
        slot = lax.broadcasted_iota(jnp.int32, (BUCKETS, 128), 1) + h * 128
        share = lax.broadcasted_iota(jnp.int32, (BUCKETS, 128), 0) * (slots // BUCKETS)
        slot = (((slot - share + slots // 2) & (slots - 1)) - slots // 2).astype(f32)
        found = [
            jnp.max(jnp.where(bucket == b, 1.0, 0.0), axis=0, keepdims=True) for b in range(BUCKETS)
        ]
        found = jnp.concatenate(found, axis=0) > 0.0
        lows.append(jnp.where(found, slot, float(slots)))
        highs.append(jnp.where(found, slot + 1.0, -float(slots)))
    low = jnp.floor(jnp.min(jnp.minimum(lows[0], lows[1]), axis=1, keepdims=True) * (1.0 / STEP))
    high = jnp.max(jnp.maximum(highs[0], highs[1]), axis=1, keepdims=True)
    rounds = (jnp.max(high - low * STEP).astype(jnp.int32) + (STEP - 1)) // STEP
    low = jnp.minimum(low, float(slots // STEP)) + float(slots // 2 // STEP)
    index = lax.broadcasted_iota(jnp.int32, (BUCKETS, 1), 0)
    weight = jnp.where(
        index % 4 == 0, 1.0, jnp.where(index % 4 == 1, 64.0, jnp.where(index % 4 == 2, 4096.0, 262144.0))
    )
    firsts = []
    for part in (0, 1):
        packed = jnp.sum(jnp.where(index // 4 == part, low * weight, 0.0)).astype(jnp.int32)
        firsts += [(packed >> (6 * n)) & 63 for n in range(4)]
    total_ref[...] = jnp.zeros_like(total_ref)
    x_ids = lax.broadcasted_iota(jnp.int32, (span, 128), 0).astype(bf16)
    l_ids = [
        (lax.broadcasted_iota(jnp.int32, (lines, 128), 0) + g * lines).astype(bf16) for g in range(GROUPS)
    ]
    zero = jnp.zeros((), bf16)
    one = jnp.ones((), bf16)

    def step(t, carry):
        for b in range(BUCKETS):
            half, group = b // GROUPS, b % GROUPS
            share = b * (slots // BUCKETS // STEP) - slots // 2 // STEP
            first = ((firsts[b] + share + t) & (slots // STEP - 1)) * STEP
            rows = pl.ds(pl.multiple_of(first, STEP), STEP)
            x_rows, l_rows = x_ref[half, rows, :], l_ref[rows, :]
            value_rows = [value_ref[c, rows, :] for c in range(8)]
            sums = None
            for pair in range(STEP // PAIR):
                xs, values = [], []
                for k in range(pair * PAIR, (pair + 1) * PAIR):
                    xs.append(jnp.where(x_ids == spread(x_rows, k, span // 16), one, zero))
                    hot = l_ids[group] == spread(l_rows, k, lines // 16)
                    parts = [
                        jnp.where(hot, spread(value_rows[c], k, lines // 16), zero) for c in range(8)
                    ]
                    values.append(jnp.concatenate(parts, axis=0))
                xs = jnp.concatenate(xs, axis=1)
                part = dot_nt(jnp.concatenate(values, axis=1), xs)
                sums = part if sums is None else sums + part
            total_ref[b] += sums
        return carry

    lax.fori_loop(0, rounds, step, 0)
    copies = []
    for c in range(1, 5):
        for half in range(HALVES):
            parts = [
                total_ref[half * GROUPS + g, (c - 1) * lines : c * lines, :]
                + total_ref[half * GROUPS + g, (c + 3) * lines : (c + 4) * lines, :]
                for g in range(GROUPS)
            ]
            deposit = jnp.concatenate(parts, axis=0).T
            here = slice(half * span, (half + 1) * span)
            done_ref[c - 1, here] = rate_ref[c, here] - deposit
        copies.append(pltpu.make_async_copy(done_ref.at[c - 1], out_ref.at[c], sems.at[c]))
        copies[-1].start()
    for copy in copies:
        copy.wait()
    mass_copy.wait()


def along(block, distance):
    count = lax.axis_size("line")
    return lax.ppermute(block, "line", [(i, (i + distance) % count) for i in range(count)])


def run_fill(
    peers, grain_holding_processor, grain_mesh_slot, grain_speed_vector, fluid_speed_at_grain,
    thermal_states, grain_mass_over_lag,
):
    parts = grain_mesh_slot.shape[0]
    blocks = parts // 128
    return pl.pallas_call(
        fill_kernel,
        name="fill",
        compiler_params=pltpu.CompilerParams(vmem_limit_bytes=60 << 20),
        out_shape=jax.ShapeDtypeStruct((peers * 10, 128), f32),
        in_specs=[pl.BlockSpec(memory_space=pltpu.HBM)] * 7,
        cost_estimate=pl.CostEstimate(flops=12 * 10**9, bytes_accessed=10**6, transcendentals=0),
        scratch_shapes=[
            pltpu.VMEM((blocks, 128), jnp.int32),
            pltpu.VMEM((blocks, 128), jnp.int32),
            pltpu.VMEM((1, parts), jnp.int32),
            pltpu.VMEM((3, parts), f32),
            pltpu.VMEM((3, parts), f32),
            pltpu.VMEM((2, parts), f32),
            pltpu.VMEM((1, parts), f32),
            pltpu.SemaphoreType.DMA((7,)),
            pltpu.VMEM((8, parts), f32),
            pltpu.VMEM((8, parts), f32),
            pltpu.VMEM((blocks, 128), f32),
            pltpu.VMEM((blocks, peers, 128), bf16),
            pltpu.VMEM((blocks, BUCKETS, peers), f32),
            pltpu.VMEM((10 * peers, 256), f32),
        ],
    )(
        grain_holding_processor.reshape(blocks, 128),
        grain_mesh_slot.reshape(blocks, 128),
        grain_mesh_slot.reshape(1, parts),
        grain_speed_vector,
        fluid_speed_at_grain,
        thermal_states,
        grain_mass_over_lag.reshape(1, parts),
    )


def run_bin(arrived, rate):
    cells, lines = rate.shape[1:]
    return pl.pallas_call(
        bin_kernel,
        name="bin",
        compiler_params=pltpu.CompilerParams(vmem_limit_bytes=20 << 20),
        out_shape=jax.ShapeDtypeStruct((5, cells, lines), f32),
        in_specs=[pl.BlockSpec(memory_space=pltpu.VMEM)] * 2,
        out_specs=pl.BlockSpec(memory_space=pltpu.HBM),
        scratch_shapes=[
            pltpu.VMEM((HALVES, 256, 128), f32),
            pltpu.VMEM((256, 128), f32),
            pltpu.VMEM((8, 256, 128), f32),
            pltpu.VMEM((BUCKETS, 8 * lines // GROUPS, cells // HALVES), f32),
            pltpu.VMEM((4, cells, lines), f32),
            pltpu.SemaphoreType.DMA((5,)),
        ],
    )(arrived, rate)


def body(
    mass_per_volume,
    fluid_speed_field,
    fluid_thrust_field,
    shock_damping_field,
    grain_holding_processor,
    grain_mesh_slot,
    grain_speed_vector,
    fluid_speed_at_grain,
    thermal_states,
    grain_mass_over_lag,
):
    cells, lines = mass_per_volume.shape
    peers = lax.axis_size(("line", "slab"))
    blocks, probe, fix = operator_tables(cells)
    outgoing = run_fill(
        peers, grain_holding_processor, grain_mesh_slot, grain_speed_vector, fluid_speed_at_grain,
        thermal_states, grain_mass_over_lag,
    )
    arrived = lax.all_to_all(
        outgoing.reshape(peers, 5, 2, 128), ("line", "slab"), split_axis=0, concat_axis=0, tiled=True
    ).reshape(peers * 10, 128)

    gas = (mass_per_volume, fluid_speed_field, fluid_thrust_field, shock_damping_field)
    own, up, down, far_up, far_down = pl.pallas_call(
        edge_kernel,
        name="edge",
        compiler_params=pltpu.CompilerParams(vmem_limit_bytes=20 << 20),
        out_shape=(
            jax.ShapeDtypeStruct((cells, lines), f32),
            jax.ShapeDtypeStruct((96, lines), f32),
            jax.ShapeDtypeStruct((96, lines), f32),
            jax.ShapeDtypeStruct((8, lines), f32),
            jax.ShapeDtypeStruct((8, lines), f32),
        ),
        cost_estimate=pl.CostEstimate(flops=10**9, bytes_accessed=2 * 10**6, transcendentals=0),
    )(*gas, blocks, probe)
    left, right = along(up, 1), along(down, -1)
    far_left, far_right = along(far_up, 2), along(far_down, -2)
    rate = pl.pallas_call(
        flux_kernel,
        name="flux",
        compiler_params=pltpu.CompilerParams(vmem_limit_bytes=20 << 20),
        out_shape=jax.ShapeDtypeStruct((5, cells, lines), f32),
        cost_estimate=pl.CostEstimate(flops=2 * 10**9, bytes_accessed=4 * 10**6, transcendentals=0),
    )(*gas, own, up, down, left, right, far_left, far_right, blocks, fix)
    return run_bin(arrived, rate)


def solution(mesh):
    placed = (
        P("line", "slab"),
        P(None, "line", "slab"),
        P("line", "slab"),
        P("line", "slab"),
        P(("line", "slab"), None),
        P(("line", "slab")),
        P(None, ("line", "slab")),
        P(None, ("line", "slab")),
        P(None, ("line", "slab")),
        P(("line", "slab")),
    )
    step = jax.shard_map(
        body, mesh=mesh, in_specs=placed, out_specs=P(None, "line", "slab"), check_vma=False
    )
    return step
```
